32 devices in a mesh: row: 4 (over x, core), col: 8 (over z, y).
Axes of the slice: x: 2, y: 2, z: 4, core: 2. Of those that a mesh axis runs over, the one named last changes fastest.
Arguments:
- blocks: float32 [256, 8, 128, 128], P(('row', 'col')), may hold values from -2 to 2
- prolong: float32 [256, 128, 128], P(('row', 'col')), may hold values from -0.5 to 0.5
- counts: int32 [256], P(('row', 'col')), may hold values from 1 to 8
- columns: int32 [256, 8], P(('row', 'col')), may hold values from 0 to 63, as said below
- aggregates: int32 [256], P(('row', 'col')), may hold values from 0 to 1
Outputs:
- coarse_operator: float32 [64, 16, 128, 128], P(('row', 'col'))
The draws below stay inside these ranges and needn't reach their ends.
Inputs may be any that keep to these rules, and one draw needn't show every extreme that they name: Over all slots of the 8 rows of one device, the columns that fall among the rows of any one device of the slab (columns // 8 equal) take at most 2 distinct values; every device reaches 2 for some such device.
All inputs are finite; a program needn't handle non-finite values.
Results may differ from the reference program's by a relative error of at most 0.0003.
Values sent between devices are 32-bit elements; how exact they have to be, the bound alone decides.
A program may use at most 64 MiB of HBM per device.

```python
import jax
import jax.numpy as jnp
from jax import lax

TB = 128
K = 8
BR = 8
AGD = 2
CAP = 2
NB = 256
N_COL = 8


def draw_columns(key, part):
    key_owner = jax.random.fold_in(key, 11)
    key_base = jax.random.fold_in(key, 12)
    key_offset = jax.random.fold_in(key, 13)
    owner = jax.random.randint(key_owner, (NB, K), 0, N_COL, dtype=jnp.int32)
    offset = jax.random.randint(key_offset, (NB, K), 0, CAP, dtype=jnp.int32)
    base = jax.random.randint(key_base, (NB // BR, N_COL), 0, BR, dtype=jnp.int32)
    base_rows = jnp.repeat(base, BR, axis=0)
    first_row = jnp.arange(NB, dtype=jnp.int32) % BR == 0
    first_slots = jnp.arange(K, dtype=jnp.int32) < CAP
    forced = first_row[:, None] & first_slots[None, :]
    owner = jnp.where(forced, owner[:, :1], owner)
    offset = jnp.where(forced, jnp.arange(K, dtype=jnp.int32)[None, :], offset)
    chosen = jnp.take_along_axis(base_rows, owner, axis=1)
    local = (chosen + offset) % BR
    return (owner * BR + local).astype(jnp.int32)


def place_ends(entries, stream_key, smallest, largest):
    longest = entries.shape.index(max(entries.shape))
    spots = []
    for shift in (0, 1):
        where = [jax.random.randint(jax.random.fold_in(stream_key, axis), (), 0, length) for axis, length in enumerate(entries.shape)]
        where[longest] = (where[longest] + shift) % entries.shape[longest]
        spots.append(tuple(where))
    return entries.at[spots[0]].set(smallest).at[spots[1]].set(largest)


def block_scale(key, dims, shards, low, top_value):
    level, own = 1.0, jax.random.fold_in(key, 6)
    for axis_at, blocks in shards:
        steps = jnp.exp(jax.random.uniform(jax.random.fold_in(own, axis_at), (blocks,), jnp.float32, low / len(shards), top_value / len(shards)))
        level = level * jnp.repeat(steps, dims[axis_at] // blocks).reshape([-1 if axis == axis_at else 1 for axis in range(len(dims))])
    return level


def bell_draw(rng, extent, width, most, pieces=(), kind=jnp.bfloat16):
    drawn = jax.random.normal(rng, extent, jnp.float32) * width
    if len(pieces) > 0:
        drawn = block_scale(rng, extent, pieces, -0.22, 0.18) * drawn
    return jnp.clip(drawn, min=-most, max=most).astype(kind)


def setup_inputs(seed: int = 0) -> dict:
    arg_keys = jax.random.split(jax.random.key(seed), 6)
    blocks = bell_draw(arg_keys[0], (NB, K, TB, TB), 0.25, 2.0, ((0, 32),), jnp.float32)
    prolong = bell_draw(arg_keys[1], (NB, TB, TB), TB ** -0.5, 0.5, ((0, 32),), jnp.float32)
    counts = place_ends(jax.random.randint(arg_keys[2], (NB,), 1, K + 1), jax.random.fold_in(arg_keys[2], 1), 1, K).astype(jnp.int32)
    columns = draw_columns(jax.random.fold_in(arg_keys[5], 71), 0)
    aggregates = place_ends(jax.random.randint(arg_keys[4], (NB,), 0, AGD), jax.random.fold_in(arg_keys[4], 1), 0, AGD - 1).astype(jnp.int32)
    return {"blocks": blocks, "prolong": prolong, "counts": counts, "columns": columns, "aggregates": aggregates}


def reference(blocks, prolong, counts, columns, aggregates):
    fine = BR * N_COL
    wide = AGD * N_COL
    slots = blocks.shape[1]
    tile = blocks.shape[-1]
    groups = blocks.shape[0] // BR
    high = lax.Precision.HIGHEST

    def one_group(group):
        start = (group * BR).astype(jnp.int32)
        tiles = lax.dynamic_slice_in_dim(blocks, start, BR, 0)
        own = lax.dynamic_slice_in_dim(prolong, start, BR, 0)
        live_count = lax.dynamic_slice_in_dim(counts, start, BR, 0)
        cols = lax.dynamic_slice_in_dim(columns, start, BR, 0)
        own_agg = lax.dynamic_slice_in_dim(aggregates, start, BR, 0)
        base = ((group // N_COL) * fine).astype(jnp.int32)
        joined = (base + cols).astype(jnp.int32)
        picked = jnp.take(prolong, joined, axis=0)
        col_agg = jnp.take(aggregates, joined, axis=0)
        coarse_col = (cols // BR) * AGD + col_agg
        inner = jnp.einsum('bkxy,bkyz->bkxz', tiles, picked, precision=high)
        terms = jnp.einsum('bxw,bkxz->bkwz', own, inner, precision=high)
        live = (jnp.arange(slots, dtype=jnp.int32)[None, :] < live_count[:, None]).astype(blocks.dtype)
        col_hot = (coarse_col[:, :, None] == jnp.arange(wide, dtype=jnp.int32)[None, None, :]).astype(blocks.dtype) * live[:, :, None]
        row_hot = (own_agg[:, None] == jnp.arange(AGD, dtype=jnp.int32)[None, :]).astype(blocks.dtype)
        weights = (row_hot[:, None, :, None] * col_hot[:, :, None, :]).reshape(BR * slots, AGD * wide)
        flat_terms = terms.reshape(BR * slots, tile * tile)
        summed = jnp.dot(weights.T, flat_terms, precision=high)
        return summed.reshape(AGD, wide, tile, tile)

    galerkin = lax.map(one_group, jnp.arange(groups, dtype=jnp.int32))
    galerkin = galerkin.reshape(groups * AGD, wide, tile, tile)
    sums = jnp.sum(jnp.abs(galerkin), axis=(1, 3))
    bound = jnp.max(sums)
    return galerkin / (bound + 1e-6)
```

```python
import functools

import jax
import jax.numpy as jnp
from jax import lax
from jax.experimental import pallas as pl
from jax.experimental.pallas import tpu as pltpu
from jax.sharding import PartitionSpec as P

AGD = 2
CAP = 2
F32 = jnp.float32
BF16 = jnp.bfloat16
I32 = jnp.int32


def halves(x):
    high = x.astype(BF16)
    return high, (x - high.astype(F32)).astype(BF16)


def dot(a, b):
    return jnp.dot(a, b, preferred_element_type=F32)


def kernel(
    n, m, blocks_ref, prolong_ref, cols_ref, agg_ref, counts_ref,
    out_ref, bound_ref,
    ask, cols_s, agg_s, counts_s, small_sem,
    blocks, prolong, partial, table, sent, got, ask_all, rowsum, peak, peaks, table_s,
    block_sem, prolong_sem, table_sem, ask_send, ask_recv,
    tile_send, tile_recv, peak_send, peak_recv, known,
):
    rows, slots = cols_s.shape
    tile = prolong.shape[-1]
    none = rows * slots
    me = lax.axis_index("col")
    my_row = lax.axis_index("row")

    width = max(1, n // 4)
    length = n // width
    line, y = me // width, lax.rem(me, width)
    side = line // (length // 2)
    inward = 1 - 2 * side

    def each(distance, first, last, act):
        for way in (1, -1) if distance else (1,):
            z = line + way * distance * inward

            @pl.when((z >= 0) & (z < length))
            def _():
                @pl.loop(first, last)
                def _(off):
                    act(z * width + lax.rem(y + off, width))

    def across(off):
        return lax.rem(me + off, n)

    def below(off):
        return lax.rem(my_row + off, m)

    barrier = pltpu.get_barrier_semaphore()

    def greet(to):
        pl.semaphore_signal(barrier, inc=1, device_id={"col": to})

    each(1, 0, 1, greet)
    each(0, 1, width, greet)

    @pl.loop(1, m)
    def _(off):
        pl.semaphore_signal(barrier, inc=1, device_id={"row": below(off)})

    beside = (line > 0).astype(I32) + (line < length - 1).astype(I32)

    small = [
        pltpu.make_async_copy(src, dst, small_sem.at[at])
        for at, (src, dst) in enumerate(
            (
                (cols_ref, ask.at[pl.ds(0, rows)]),
                (agg_ref, ask.at[pl.ds(rows, 1)]),
                (cols_ref, cols_s),
                (agg_ref, agg_s),
                (counts_ref, counts_s),
            )
        )
    ]
    load_prolong = pltpu.make_async_copy(prolong_ref, prolong, prolong_sem)
    for copy in small:
        copy.start()
    load_prolong.start()

    def load_block(i):
        return pltpu.make_async_copy(blocks_ref.at[i], blocks.at[i], block_sem.at[i])

    @pl.loop(0, rows)
    def _(i):
        load_block(i).start()

    for copy in small:
        copy.wait()
    pl.semaphore_wait(barrier, beside + width - 1 + m - 1)

    def send_ask(to, slot):
        return pltpu.make_async_remote_copy(
            ask, ask_all.at[slot], ask_send.at[to], ask_recv.at[slot], device_id={"col": to}
        )

    def send_tiles(to, slot):
        return pltpu.make_async_remote_copy(
            sent.at[to], got.at[slot], tile_send.at[to], tile_recv.at[slot], device_id={"col": to}
        )

    def ask_for(to):
        send_ask(to, me).start()

    def tell():
        @pl.when(line > 0)
        def _():
            pl.semaphore_signal(known.at[1], inc=1, device_id={"col": me - width})

        @pl.when(line < length - 1)
        def _():
            pl.semaphore_signal(known.at[0], inc=1, device_id={"col": me + width})

    def hear():
        @pl.when(line > 0)
        def _():
            pl.semaphore_wait(known.at[0], 1)

        @pl.when(line < length - 1)
        def _():
            pl.semaphore_wait(known.at[1], 1)

    tell()
    each(1, 0, 1, ask_for)
    each(0, 1, width, ask_for)
    for distance in range(1, length):
        hear()
        if distance < length - 1:
            tell()
        each(distance, 1, width, ask_for)
        if distance < length - 1:
            each(distance + 1, 0, 1, ask_for)

    load_prolong.wait()

    def reply(to):
        send_ask(to, to).wait_recv()
        asked = ask_all[to][:rows]
        mine = asked // rows == me
        within = lax.rem(asked, rows)
        sent[to, 0] = prolong[jnp.min(jnp.where(mine, within, rows - 1))]
        sent[to, 1] = prolong[jnp.max(jnp.where(mine, within, 0))]
        send_tiles(to, me).start()

    each(0, 1, width, reply)
    for distance in range(1, length):
        each(distance, 0, 1, reply)
        each(distance, 1, width, reply)

    sub = lax.broadcasted_iota(I32, (8, 128), 0)
    lane = lax.broadcasted_iota(I32, (8, 128), 1)
    keys = jnp.full((8, 128), -1, I32)
    for i in range(rows):
        for k in range(slots):
            here = (sub == i) & (lane == k)
            keys = jnp.where(here, cols_s[i, k] * AGD + agg_s[0, i], keys)
    order = sub * slots + lane

    def scan_keys(i, carry):
        prev, low, high = carry
        for k in range(slots):
            col = cols_s[i, k]
            s = i * slots + k
            owner, within = col // rows, lax.rem(col, rows)
            key = jnp.where(k < counts_s[0, i], col * AGD + agg_s[0, i], -2)
            prev = jnp.where((keys == key) & (order > s), s, prev)
            low = jnp.where(lane == owner, jnp.minimum(low, within), low)
            high = jnp.where(lane == owner, jnp.maximum(high, within), high)
        return prev, low, high

    prev, low, high = lax.fori_loop(
        0, rows, scan_keys,
        (jnp.full((8, 128), none, I32), jnp.full((8, 128), rows - 1, I32), jnp.zeros((8, 128), I32)),
    )
    wanted = jnp.where(lax.rem(sub, 2) == 0, low, jnp.where(high > low, high, -1))

    def scan_last(i, last):
        for k in range(slots):
            col = cols_s[i, k]
            owner, within = col // rows, lax.rem(col, rows)
            row = jnp.where(k < counts_s[0, i], agg_s[0, i], -1)
            hit = (lane == owner) & (sub // 2 == row) & (wanted == within)
            last = jnp.where(hit, i * slots + k, last)
        return last

    last = lax.fori_loop(0, rows, scan_last, jnp.full((8, 128), none, I32))
    table[0:8, :] = prev
    table[8:16, :] = last
    table[16:24, :] = jnp.where(sub == 0, low, high)
    to_scalars = pltpu.make_async_copy(table, table_s, table_sem)
    to_scalars.start()
    partial[none] = jnp.zeros((tile, tile), F32)
    ask_all[me] = ask[...]
    rowsum[...] = jnp.zeros_like(rowsum)
    to_scalars.wait()

    got[me, 0] = prolong[table_s[16, me]]
    got[me, 1] = prolong[table_s[17, me]]

    def first_product(i, _):
        load_block(i).wait()
        ph, pw = halves(prolong[i].T)
        lhs = jnp.concatenate([ph, pw, ph], axis=1)
        for k in range(0, slots, 2):
            ah, aw = halves(blocks[i, k])
            bh, bw = halves(blocks[i, k + 1])
            highs = jnp.concatenate([ah, bh], axis=1)
            rhs = jnp.concatenate([highs, highs, jnp.concatenate([aw, bw], axis=1)], axis=0)
            both = dot(lhs, rhs)
            s = i * slots + k
            partial[s] = both[:, :tile] + partial[table_s[i, k]]
            partial[s + 1] = both[:, tile:] + partial[table_s[i, k + 1]]
        return 0

    lax.fori_loop(0, rows, first_product, 0)

    spot = lax.broadcasted_iota(I32, (1, rows), 1)

    def second_product(owner):
        lhs = jnp.concatenate(
            [
                jnp.concatenate([partial[table_s[8 + c * CAP + r, owner]] for r in range(CAP)], axis=1)
                for c in range(AGD)
            ],
            axis=0,
        )
        ids = ask_all[owner][rows:]
        right = []
        for r in range(CAP):
            one = jnp.max(jnp.where(spot == table_s[16 + r, owner], ids, 0)).astype(F32)
            p = got[owner, r]
            right.append(jnp.concatenate([p * (1.0 - one), p * one], axis=1))
        rhs = jnp.concatenate(right, axis=0)
        lh, lw = halves(lhs)
        rh, rw = halves(rhs)
        prod = dot(lh, rh) + dot(lh, rw) + dot(lw, rh)
        size = jnp.abs(prod)
        rowsum[...] += size[:, :tile] + size[:, tile:]
        for c in range(AGD):
            for a in range(AGD):
                out_ref[c, owner * AGD + a] = prod[
                    c * tile : (c + 1) * tile, a * tile : (a + 1) * tile
                ]

    second_product(me)

    def collect(owner):
        send_tiles(owner, owner).wait_recv()
        second_product(owner)

    @pl.loop(1, n)
    def _(t):
        far = t // width
        own = line // (length // 2) * (length // 2)
        z = jnp.where(
            far < length // 2,
            own + lax.rem(line - own + far, length // 2),
            jnp.where(side == 0, length - 1 - (far - length // 2), far - length // 2),
        )
        collect(z * width + lax.rem(y + t, width))

    most = jnp.max(jnp.sum(rowsum[...], axis=1, keepdims=True), axis=0, keepdims=True)
    place_all = my_row * n + me
    peak[...] = jnp.broadcast_to(most, peak.shape)
    peaks[place_all] = jnp.broadcast_to(most, peak.shape)

    def far_first(t):
        down = n - t - (n - t <= me).astype(I32)
        return jnp.where(side == 0, down, t - 1 + (t - 1 >= me).astype(I32))

    def send_peak(row, col):
        return pltpu.make_async_remote_copy(
            peak, peaks.at[place_all], peak_send, peak_recv, device_id={"row": row, "col": col}
        )

    @pl.loop(1, n)
    def _(t):
        @pl.loop(0, m)
        def _(off):
            send_peak(below(off), far_first(t)).start()

    @pl.loop(1, m)
    def _(off):
        send_peak(below(off), me).start()

    @pl.loop(1, n)
    def _(off):
        to = across(off)
        send_ask(to, me).wait_send()
        send_tiles(to, me).wait_send()

    others = pl.ds(0, n * m - 1)
    every = pltpu.make_async_remote_copy(
        peaks.at[others], peaks.at[others], peak_send, peak_recv, device_id={"col": across(1)}
    )
    every.wait_send()
    every.wait_recv()
    bound_ref[...] = jnp.broadcast_to(
        jnp.max(peaks[...], axis=0)[:1, :1] + 1e-06, bound_ref.shape
    )


def per_device(blocks, prolong, counts, columns, aggregates):
    rows, slots, tile, _ = blocks.shape
    n, m = lax.axis_size("col"), lax.axis_size("row")
    agg_row = aggregates.reshape(1, rows)
    dma = pltpu.SemaphoreType.DMA
    vmem = pl.BlockSpec(memory_space=pltpu.VMEM)
    hbm = pl.BlockSpec(memory_space=pltpu.HBM)
    galerkin, bound = pl.pallas_call(
        functools.partial(kernel, n, m),
        name="galerkin",
        out_shape=(
            jax.ShapeDtypeStruct((AGD, AGD * n, tile, tile), F32),
            jax.ShapeDtypeStruct((tile, tile), F32),
        ),
        in_specs=[hbm] * 5,
        out_specs=(vmem, vmem),
        scratch_shapes=[
            pltpu.VMEM((rows + 1, slots), I32),
            pltpu.SMEM((rows, slots), I32),
            pltpu.SMEM((1, rows), I32),
            pltpu.SMEM((1, rows), I32),
            dma((5,)),
            pltpu.VMEM((rows, slots, tile, tile), F32),
            pltpu.VMEM((rows, tile, tile), F32),
            pltpu.VMEM((rows * slots + 1, tile, tile), F32),
            pltpu.VMEM((24, 128), I32),
            pltpu.VMEM((n, CAP, tile, tile), F32),
            pltpu.VMEM((n, CAP, tile, tile), F32),
            pltpu.VMEM((n, rows + 1, slots), I32),
            pltpu.VMEM((AGD * tile, tile), F32),
            pltpu.VMEM((1, 128), F32),
            pltpu.VMEM((n * m, 1, 128), F32),
            pltpu.SMEM((24, 128), I32),
            dma((rows,)),
            dma,
            dma,
            dma((n,)),
            dma((n,)),
            dma((n,)),
            dma((n,)),
            dma,
            dma,
            pltpu.SemaphoreType.REGULAR((2,)),
        ],
        compiler_params=pltpu.CompilerParams(
            collective_id=0, has_side_effects=True, vmem_limit_bytes=48 * 1024 * 1024
        ),
    )(*(pltpu.with_memory_space_constraint(x, pltpu.HBM) for x in (blocks, prolong, columns, agg_row, counts.reshape(1, rows))))
    return galerkin / bound


def solution(mesh):
    placed = (
        P(("row", "col"), None, None, None),
        P(("row", "col"), None, None),
        P(("row", "col")),
        P(("row", "col"), None),
        P(("row", "col")),
    )
    return jax.shard_map(
        per_device,
        mesh=mesh,
        in_specs=placed,
        out_specs=P(("row", "col"), None, None, None),
        check_vma=False,
    )
```

```python
import functools

import jax
import jax.numpy as jnp
from jax import lax
from jax.experimental import pallas as pl
from jax.experimental.pallas import tpu as pltpu
from jax.sharding import PartitionSpec as P

AGD = 2
CAP = 2
F32 = jnp.float32
BF16 = jnp.bfloat16
I32 = jnp.int32


def halves(x):
    high = x.astype(BF16)
    return high, (x - high.astype(F32)).astype(BF16)


def dot(a, b):
    return jnp.dot(a, b, preferred_element_type=F32)


def kernel(
    n, m, blocks_ref, prolong_ref, cols_ref, agg_ref, counts_ref,
    out_ref, bound_ref,
    ask, cols_s, agg_s, counts_s, small_sem,
    blocks, prolong, partial, table, sent, got, pushed, passed, ask_all, rowsum, peak, peaks, table_s,
    block_sem, prolong_sem, table_sem, ask_send, ask_recv,
    tile_send, tile_recv, relay_send, relay_recv, push_send, push_recv,
    peak_send, peak_recv, known,
):
    rows, slots = cols_s.shape
    tile = prolong.shape[-1]
    none = rows * slots
    cut = tile * 3 // 8
    lead = tile // 4
    me = lax.axis_index("col")
    my_row = lax.axis_index("row")

    width = n // 4
    line, y = me // width, lax.rem(me, width)
    side = line // 2
    outer = lax.rem(line + side, 2) == 0
    inner = lax.rem(line + side, 2) == 1

    def own(far, off):
        return jnp.where(side == 1, 2 + far, 1 - far) * width + lax.rem(y + off, width)

    def facing(far, off):
        return jnp.where(side == 1, 1 - far, 2 + far) * width + lax.rem(y + off, width)

    def across(off):
        return lax.rem(me + off, n)

    def below(off):
        return lax.rem(my_row + off, m)

    def each(where, far, first, act):
        @pl.loop(first, width)
        def _(off):
            act(where(far, off))

    barrier = pltpu.get_barrier_semaphore()

    def greet(to):
        pl.semaphore_signal(barrier, inc=1, device_id={"col": to})

    @pl.when(inner)
    def _():
        greet(facing(0, 0))
        greet(own(1, 0))

    @pl.loop(1, width)
    def _(off):
        greet(line * width + lax.rem(y + off, width))

    @pl.loop(1, m)
    def _(off):
        pl.semaphore_signal(barrier, inc=1, device_id={"row": below(off)})

    small = [
        pltpu.make_async_copy(src, dst, small_sem.at[at])
        for at, (src, dst) in enumerate(
            (
                (cols_ref, ask.at[pl.ds(0, rows)]),
                (agg_ref, ask.at[pl.ds(rows, 1)]),
                (cols_ref, cols_s),
                (agg_ref, agg_s),
                (counts_ref, counts_s),
            )
        )
    ]
    load_prolong = pltpu.make_async_copy(prolong_ref, prolong, prolong_sem)
    load_prolong.start()
    for copy in small:
        copy.start()

    def load_block(i):
        return pltpu.make_async_copy(blocks_ref.at[i], blocks.at[i], block_sem.at[i])

    def send_ask(to, slot):
        return pltpu.make_async_remote_copy(
            ask, ask_all.at[slot], ask_send.at[to], ask_recv.at[slot], device_id={"col": to}
        )

    def send_push(part):
        some = (pl.ds(0, lead), pl.ds(lead, cut - lead))[part]
        return pltpu.make_async_remote_copy(
            prolong_ref.at[:, some], pushed.at[:, some], push_send.at[part], push_recv.at[part],
            device_id={"col": facing(0, 0)},
        )

    def send_tiles(to, slot):
        return pltpu.make_async_remote_copy(
            sent.at[to], got.at[slot], tile_send.at[to], tile_recv.at[slot], device_id={"col": to}
        )

    def send_rest(to, slot):
        rest = pl.ds(cut, tile - cut)
        return pltpu.make_async_remote_copy(
            sent.at[to, :, rest], got.at[slot, :, rest], tile_send.at[to], tile_recv.at[slot],
            device_id={"col": to},
        )

    def send_relay(to, slot):
        return pltpu.make_async_remote_copy(
            passed.at[to], got.at[slot, :, pl.ds(0, cut)], relay_send.at[to], relay_recv.at[slot],
            device_id={"col": to},
        )

    def ask_for(to):
        send_ask(to, me).start()

    def tell(to, at):
        pl.semaphore_signal(known.at[at], inc=1, device_id={"col": to})

    pl.semaphore_wait(barrier, width + m - 1)

    @pl.when(inner)
    def _():
        tell(facing(0, 0), 1)
        send_push(0).start()

    @pl.when(outer)
    def _():
        tell(own(0, 0), 0)

    for copy in small:
        copy.wait()

    @pl.when(inner)
    def _():
        ask_for(facing(0, 0))
        each(own, 0, 1, ask_for)
        pl.semaphore_wait(known.at[0], 1)
        tell(facing(0, 0), 1)
        tell(own(1, 0), 0)
        each(own, 1, 0, ask_for)
        pl.semaphore_wait(known.at[1], 1)
        tell(own(1, 0), 0)
        each(facing, 0, 1, ask_for)
        pl.semaphore_wait(known.at[1], 1)
        tell(own(1, 0), 0)
        each(facing, 1, 0, ask_for)
        send_push(1).start()

    @pl.when(outer)
    def _():
        ask_for(own(0, 0))
        each(own, 1, 1, ask_for)
        pl.semaphore_wait(known.at[0], 1)
        ask_for(facing(0, 0))
        each(own, 0, 1, ask_for)
        pl.semaphore_wait(known.at[0], 1)
        each(facing, 0, 1, ask_for)
        pl.semaphore_wait(known.at[0], 1)
        each(facing, 1, 0, ask_for)

    @pl.loop(0, rows)
    def _(i):
        load_block(i).start()

    load_prolong.wait()

    def bounds(to, owner):
        asked = ask_all[to][:rows]
        mine = asked // rows == owner
        within = lax.rem(asked, rows)
        return jnp.min(jnp.where(mine, within, rows - 1)), jnp.max(jnp.where(mine, within, 0))

    def reply(to):
        send_ask(to, to).wait_recv()
        low, high = bounds(to, me)
        sent[to, 0] = prolong[low]
        sent[to, 1] = prolong[high]
        send_tiles(to, me).start()

    def reply_rest(to):
        send_ask(to, to).wait_recv()
        low, high = bounds(to, me)
        sent[to, 0, cut:] = prolong[low][cut:]
        sent[to, 1, cut:] = prolong[high][cut:]
        send_rest(to, me).start()

    @pl.when(inner)
    def _():
        each(own, 0, 1, reply)
        each(own, 1, 0, reply)
        each(facing, 1, 0, reply_rest)
        each(facing, 0, 0, reply_rest)

    @pl.when(outer)
    def _():
        each(own, 1, 1, reply)
        each(own, 0, 0, reply)
        each(facing, 1, 0, reply)
        each(facing, 0, 0, reply)

    sub = lax.broadcasted_iota(I32, (8, 128), 0)
    lane = lax.broadcasted_iota(I32, (8, 128), 1)
    keys = jnp.full((8, 128), -1, I32)
    for i in range(rows):
        for k in range(slots):
            here = (sub == i) & (lane == k)
            keys = jnp.where(here, cols_s[i, k] * AGD + agg_s[0, i], keys)
    order = sub * slots + lane

    def scan_keys(i, carry):
        prev, low, high = carry
        for k in range(slots):
            col = cols_s[i, k]
            s = i * slots + k
            owner, within = col // rows, lax.rem(col, rows)
            key = jnp.where(k < counts_s[0, i], col * AGD + agg_s[0, i], -2)
            prev = jnp.where((keys == key) & (order > s), s, prev)
            low = jnp.where(lane == owner, jnp.minimum(low, within), low)
            high = jnp.where(lane == owner, jnp.maximum(high, within), high)
        return prev, low, high

    prev, low, high = lax.fori_loop(
        0, rows, scan_keys,
        (jnp.full((8, 128), none, I32), jnp.full((8, 128), rows - 1, I32), jnp.zeros((8, 128), I32)),
    )
    wanted = jnp.where(lax.rem(sub, 2) == 0, low, jnp.where(high > low, high, -1))

    def scan_last(i, last):
        for k in range(slots):
            col = cols_s[i, k]
            owner, within = col // rows, lax.rem(col, rows)
            row = jnp.where(k < counts_s[0, i], agg_s[0, i], -1)
            hit = (lane == owner) & (sub // 2 == row) & (wanted == within)
            last = jnp.where(hit, i * slots + k, last)
        return last

    last = lax.fori_loop(0, rows, scan_last, jnp.full((8, 128), none, I32))
    table[0:8, :] = prev
    table[8:16, :] = last
    table[16:24, :] = jnp.where(sub == 0, low, high)
    to_scalars = pltpu.make_async_copy(table, table_s, table_sem)
    to_scalars.start()
    partial[none] = jnp.zeros((tile, tile), F32)
    ask_all[me] = ask[...]
    rowsum[...] = jnp.zeros_like(rowsum)
    to_scalars.wait()

    got[me, 0] = prolong[table_s[16, me]]
    got[me, 1] = prolong[table_s[17, me]]

    @pl.when(inner)
    def _():
        send_push(0).wait_recv()
        send_push(1).wait_recv()
        face = facing(0, 0)

        def relay(to):
            low, high = bounds(to, face)
            passed[to, 0] = pushed[low]
            passed[to, 1] = pushed[high]
            send_relay(to, face).start()

        each(own, 0, 1, relay)
        each(own, 1, 0, relay)
        got[face, 0, :cut] = pushed[table_s[16, face]]
        got[face, 1, :cut] = pushed[table_s[17, face]]

    def first_product(i, _):
        load_block(i).wait()
        ph, pw = halves(prolong[i].T)
        lhs = jnp.concatenate([ph, pw, ph], axis=1)
        for k in range(0, slots, 2):
            ah, aw = halves(blocks[i, k])
            bh, bw = halves(blocks[i, k + 1])
            highs = jnp.concatenate([ah, bh], axis=1)
            rhs = jnp.concatenate([highs, highs, jnp.concatenate([aw, bw], axis=1)], axis=0)
            both = dot(lhs, rhs)
            s = i * slots + k
            partial[s] = both[:, :tile] + partial[table_s[i, k]]
            partial[s + 1] = both[:, tile:] + partial[table_s[i, k + 1]]
        return 0

    lax.fori_loop(0, rows, first_product, 0)

    spot = lax.broadcasted_iota(I32, (1, rows), 1)

    def second_product(owner):
        lhs = jnp.concatenate(
            [
                jnp.concatenate([partial[table_s[8 + c * CAP + r, owner]] for r in range(CAP)], axis=1)
                for c in range(AGD)
            ],
            axis=0,
        )
        ids = ask_all[owner][rows:]
        right = []
        for r in range(CAP):
            one = jnp.max(jnp.where(spot == table_s[16 + r, owner], ids, 0)).astype(F32)
            p = got[owner, r]
            right.append(jnp.concatenate([p * (1.0 - one), p * one], axis=1))
        rhs = jnp.concatenate(right, axis=0)
        lh, lw = halves(lhs)
        rh, rw = halves(rhs)
        prod = dot(lh, rh) + dot(lh, rw) + dot(lw, rh)
        size = jnp.abs(prod)
        rowsum[...] += size[:, :tile] + size[:, tile:]
        for c in range(AGD):
            for a in range(AGD):
                out_ref[c, owner * AGD + a] = prod[
                    c * tile : (c + 1) * tile, a * tile : (a + 1) * tile
                ]

    second_product(me)

    def collect(owner):
        send_tiles(owner, owner).wait_recv()
        second_product(owner)

    def collect_parts(owner):
        send_relay(owner, owner).wait_recv()
        send_rest(owner, owner).wait_recv()
        second_product(owner)

    @pl.when(inner)
    def _():
        each(own, 0, 1, collect)
        each(own, 1, 0, collect)

    @pl.when(outer)
    def _():
        each(own, 1, 1, collect)
        each(own, 0, 0, collect)

    each(facing, 1, 0, collect)

    @pl.when(inner)
    def _():
        send_rest(facing(0, 0), facing(0, 0)).wait_recv()

    @pl.when(outer)
    def _():
        send_relay(facing(0, 0), facing(0, 0)).wait_recv()
        send_rest(facing(0, 0), facing(0, 0)).wait_recv()

    second_product(facing(0, 0))
    each(facing, 0, 1, collect_parts)

    most = jnp.max(jnp.sum(rowsum[...], axis=1, keepdims=True), axis=0, keepdims=True)
    place_all = my_row * n + me
    peak[...] = jnp.broadcast_to(most, peak.shape)
    peaks[place_all] = jnp.broadcast_to(most, peak.shape)

    def far_first(t):
        down = n - t - (n - t <= me).astype(I32)
        return jnp.where(side == 0, down, t - 1 + (t - 1 >= me).astype(I32))

    def send_peak(row, col):
        return pltpu.make_async_remote_copy(
            peak, peaks.at[place_all], peak_send, peak_recv, device_id={"row": row, "col": col}
        )

    @pl.loop(1, n)
    def _(t):
        @pl.loop(0, m)
        def _(off):
            send_peak(below(off), far_first(t)).start()

    @pl.loop(1, m)
    def _(off):
        send_peak(below(off), me).start()

    others = pl.ds(0, n * m - 1)
    every = pltpu.make_async_remote_copy(
        peaks.at[others], peaks.at[others], peak_send, peak_recv, device_id={"col": across(1)}
    )

    @pl.loop(1, n)
    def _(off):
        send_ask(across(off), me).wait_send()

    def sent_whole(to):
        send_tiles(to, me).wait_send()

    def sent_rest(to):
        send_rest(to, me).wait_send()

    def sent_relay(to):
        send_relay(to, me).wait_send()

    @pl.when(inner)
    def _():
        send_push(0).wait_send()
        send_push(1).wait_send()
        each(own, 0, 1, sent_whole)
        each(own, 0, 1, sent_relay)
        each(own, 1, 0, sent_whole)
        each(own, 1, 0, sent_relay)
        each(facing, 0, 0, sent_rest)
        each(facing, 1, 0, sent_rest)

    @pl.when(outer)
    def _():
        each(own, 1, 1, sent_whole)
        each(own, 0, 0, sent_whole)
        each(facing, 0, 0, sent_whole)
        each(facing, 1, 0, sent_whole)

    every.wait_recv()
    bound_ref[...] = jnp.broadcast_to(
        jnp.max(peaks[...], axis=0)[:1, :1] + 1e-06, bound_ref.shape
    )
    every.wait_send()


def per_device(blocks, prolong, counts, columns, aggregates):
    rows, slots, tile, _ = blocks.shape
    n, m = lax.axis_size("col"), lax.axis_size("row")
    agg_row = aggregates.reshape(1, rows)
    dma = pltpu.SemaphoreType.DMA
    vmem = pl.BlockSpec(memory_space=pltpu.VMEM)
    hbm = pl.BlockSpec(memory_space=pltpu.HBM)
    galerkin, bound = pl.pallas_call(
        functools.partial(kernel, n, m),
        name="galerkin",
        out_shape=(
            jax.ShapeDtypeStruct((AGD, AGD * n, tile, tile), F32),
            jax.ShapeDtypeStruct((tile, tile), F32),
        ),
        in_specs=[hbm] * 5,
        out_specs=(vmem, vmem),
        scratch_shapes=[
            pltpu.VMEM((rows + 1, slots), I32),
            pltpu.SMEM((rows, slots), I32),
            pltpu.SMEM((1, rows), I32),
            pltpu.SMEM((1, rows), I32),
            dma((5,)),
            pltpu.VMEM((rows, slots, tile, tile), F32),
            pltpu.VMEM((rows, tile, tile), F32),
            pltpu.VMEM((rows * slots + 1, tile, tile), F32),
            pltpu.VMEM((24, 128), I32),
            pltpu.VMEM((n, CAP, tile, tile), F32),
            pltpu.VMEM((n, CAP, tile, tile), F32),
            pltpu.VMEM((rows, tile * 3 // 8, tile), F32),
            pltpu.VMEM((n, CAP, tile * 3 // 8, tile), F32),
            pltpu.VMEM((n, rows + 1, slots), I32),
            pltpu.VMEM((AGD * tile, tile), F32),
            pltpu.VMEM((1, 128), F32),
            pltpu.VMEM((n * m, 1, 128), F32),
            pltpu.SMEM((24, 128), I32),
            dma((rows,)),
            dma,
            dma,
            dma((n,)),
            dma((n,)),
            dma((n,)),
            dma((n,)),
            dma((n,)),
            dma((n,)),
            dma((2,)),
            dma((2,)),
            dma,
            dma,
            pltpu.SemaphoreType.REGULAR((2,)),
        ],
        compiler_params=pltpu.CompilerParams(
            collective_id=0, has_side_effects=True, vmem_limit_bytes=48 * 1024 * 1024
        ),
    )(*(pltpu.with_memory_space_constraint(x, pltpu.HBM) for x in (blocks, prolong, columns, agg_row, counts.reshape(1, rows))))
    return galerkin / bound


def solution(mesh):
    placed = (
        P(("row", "col"), None, None, None),
        P(("row", "col"), None, None),
        P(("row", "col")),
        P(("row", "col"), None),
        P(("row", "col")),
    )
    return jax.shard_map(
        per_device,
        mesh=mesh,
        in_specs=placed,
        out_specs=P(("row", "col"), None, None, None),
        check_vma=False,
    )
```

```python
import functools

import jax
import jax.numpy as jnp
from jax import lax
from jax.experimental import pallas as pl
from jax.experimental.pallas import tpu as pltpu
from jax.sharding import PartitionSpec as P

AGD = 2
CAP = 2
F32 = jnp.float32
BF16 = jnp.bfloat16
I32 = jnp.int32


def halves(x):
    high = x.astype(BF16)
    return high, (x - high.astype(F32)).astype(BF16)


def dot(a, b):
    return jnp.dot(a, b, preferred_element_type=F32)


def kernel(
    n, m, blocks_ref, prolong_ref, cols_ref, agg_ref, counts_ref,
    out_ref, bound_ref,
    ask, cols_s, agg_s, counts_s, small_sem,
    blocks, prolong, partial, table, sent, got, pushed, passed, ask_all, rowsum, peak, peaks, table_s,
    block_sem, prolong_sem, table_sem, ask_send, ask_recv,
    tile_send, tile_recv, relay_send, relay_recv, push_send, push_recv,
    peak_send, peak_recv, known,
):
    rows, slots = cols_s.shape
    tile = prolong.shape[-1]
    none = rows * slots
    cut = tile // 2
    lead = tile // 4
    me = lax.axis_index("col")
    my_row = lax.axis_index("row")

    width = n // 4
    line, y = me // width, lax.rem(me, width)
    side = line // 2
    outer = lax.rem(line + side, 2) == 0
    inner = lax.rem(line + side, 2) == 1

    def own(far, off):
        return jnp.where(side == 1, 2 + far, 1 - far) * width + lax.rem(y + off, width)

    def facing(far, off):
        return jnp.where(side == 1, 1 - far, 2 + far) * width + lax.rem(y + off, width)

    def across(off):
        return lax.rem(me + off, n)

    def below(off):
        return lax.rem(my_row + off, m)

    def each(where, far, first, act):
        @pl.loop(first, width)
        def _(off):
            act(where(far, off))

    barrier = pltpu.get_barrier_semaphore()

    def greet(to):
        pl.semaphore_signal(barrier, inc=1, device_id={"col": to})

    @pl.when(inner)
    def _():
        greet(facing(0, 0))
        greet(own(1, 0))

    @pl.loop(1, width)
    def _(off):
        greet(line * width + lax.rem(y + off, width))

    @pl.loop(1, m)
    def _(off):
        pl.semaphore_signal(barrier, inc=1, device_id={"row": below(off)})

    small = [
        pltpu.make_async_copy(src, dst, small_sem.at[at])
        for at, (src, dst) in enumerate(
            (
                (cols_ref, ask.at[pl.ds(0, rows)]),
                (agg_ref, ask.at[pl.ds(rows, 1)]),
                (cols_ref, cols_s),
                (agg_ref, agg_s),
                (counts_ref, counts_s),
            )
        )
    ]
    load_prolong = pltpu.make_async_copy(prolong_ref, prolong, prolong_sem)
    load_prolong.start()
    for copy in small:
        copy.start()

    def load_block(i):
        return pltpu.make_async_copy(blocks_ref.at[i], blocks.at[i], block_sem.at[i])

    def send_ask(to, slot):
        return pltpu.make_async_remote_copy(
            ask, ask_all.at[slot], ask_send.at[to], ask_recv.at[slot], device_id={"col": to}
        )

    def send_push(part):
        some = (pl.ds(0, lead), pl.ds(lead, cut - lead))[part]
        return pltpu.make_async_remote_copy(
            prolong.at[:, some], pushed.at[:, some], push_send.at[part], push_recv.at[part],
            device_id={"col": facing(0, 0)},
        )

    def send_tiles(to, slot):
        return pltpu.make_async_remote_copy(
            sent.at[to], got.at[slot], tile_send.at[to], tile_recv.at[slot], device_id={"col": to}
        )

    def send_rest(to, slot):
        rest = pl.ds(cut, tile - cut)
        return pltpu.make_async_remote_copy(
            sent.at[to, :, rest], got.at[slot, :, rest], tile_send.at[to], tile_recv.at[slot],
            device_id={"col": to},
        )

    def send_relay(to, slot):
        return pltpu.make_async_remote_copy(
            passed.at[to], got.at[slot, :, pl.ds(0, cut)], relay_send.at[to], relay_recv.at[slot],
            device_id={"col": to},
        )

    def ask_for(to):
        send_ask(to, me).start()

    def tell(to, at):
        pl.semaphore_signal(known.at[at], inc=1, device_id={"col": to})

    pl.semaphore_wait(barrier, width + m - 1)

    @pl.when(inner)
    def _():
        tell(facing(0, 0), 1)
        load_prolong.wait()
        send_push(0).start()

    @pl.when(outer)
    def _():
        tell(own(0, 0), 0)

    for copy in small:
        copy.wait()

    @pl.when(inner)
    def _():
        ask_for(facing(0, 0))
        each(own, 0, 1, ask_for)
        pl.semaphore_wait(known.at[0], 1)
        tell(facing(0, 0), 1)
        tell(own(1, 0), 0)
        each(own, 1, 0, ask_for)
        pl.semaphore_wait(known.at[1], 1)
        tell(own(1, 0), 0)
        each(facing, 0, 1, ask_for)
        pl.semaphore_wait(known.at[1], 1)
        tell(own(1, 0), 0)
        each(facing, 1, 0, ask_for)
        send_push(1).start()

    @pl.when(outer)
    def _():
        ask_for(own(0, 0))
        each(own, 1, 1, ask_for)
        pl.semaphore_wait(known.at[0], 1)
        ask_for(facing(0, 0))
        each(own, 0, 1, ask_for)
        pl.semaphore_wait(known.at[0], 1)
        each(facing, 0, 1, ask_for)
        pl.semaphore_wait(known.at[0], 1)
        each(facing, 1, 0, ask_for)

    @pl.loop(0, rows)
    def _(i):
        load_block(i).start()

    @pl.when(outer)
    def _():
        load_prolong.wait()

    def bounds(to, owner):
        asked = ask_all[to][:rows]
        mine = asked // rows == owner
        within = lax.rem(asked, rows)
        return jnp.min(jnp.where(mine, within, rows - 1)), jnp.max(jnp.where(mine, within, 0))

    def reply(to):
        send_ask(to, to).wait_recv()
        low, high = bounds(to, me)
        sent[to, 0] = prolong[low]
        sent[to, 1] = prolong[high]
        send_tiles(to, me).start()

    def reply_rest(to):
        send_ask(to, to).wait_recv()
        low, high = bounds(to, me)
        sent[to, 0, cut:] = prolong[low][cut:]
        sent[to, 1, cut:] = prolong[high][cut:]
        send_rest(to, me).start()

    @pl.when(inner)
    def _():
        each(own, 0, 1, reply)
        each(own, 1, 0, reply)
        each(facing, 1, 0, reply_rest)
        each(facing, 0, 0, reply_rest)

    @pl.when(outer)
    def _():
        each(own, 1, 1, reply)
        each(own, 0, 0, reply)
        each(facing, 1, 0, reply)
        each(facing, 0, 0, reply)

    sub = lax.broadcasted_iota(I32, (8, 128), 0)
    lane = lax.broadcasted_iota(I32, (8, 128), 1)
    keys = jnp.full((8, 128), -1, I32)
    for i in range(rows):
        for k in range(slots):
            here = (sub == i) & (lane == k)
            keys = jnp.where(here, cols_s[i, k] * AGD + agg_s[0, i], keys)
    order = sub * slots + lane

    def scan_keys(i, carry):
        prev, low, high = carry
        for k in range(slots):
            col = cols_s[i, k]
            s = i * slots + k
            owner, within = col // rows, lax.rem(col, rows)
            key = jnp.where(k < counts_s[0, i], col * AGD + agg_s[0, i], -2)
            prev = jnp.where((keys == key) & (order > s), s, prev)
            low = jnp.where(lane == owner, jnp.minimum(low, within), low)
            high = jnp.where(lane == owner, jnp.maximum(high, within), high)
        return prev, low, high

    prev, low, high = lax.fori_loop(
        0, rows, scan_keys,
        (jnp.full((8, 128), none, I32), jnp.full((8, 128), rows - 1, I32), jnp.zeros((8, 128), I32)),
    )
    wanted = jnp.where(lax.rem(sub, 2) == 0, low, jnp.where(high > low, high, -1))

    def scan_last(i, last):
        for k in range(slots):
            col = cols_s[i, k]
            owner, within = col // rows, lax.rem(col, rows)
            row = jnp.where(k < counts_s[0, i], agg_s[0, i], -1)
            hit = (lane == owner) & (sub // 2 == row) & (wanted == within)
            last = jnp.where(hit, i * slots + k, last)
        return last

    last = lax.fori_loop(0, rows, scan_last, jnp.full((8, 128), none, I32))
    table[0:8, :] = prev
    table[8:16, :] = last
    table[16:24, :] = jnp.where(sub == 0, low, high)
    to_scalars = pltpu.make_async_copy(table, table_s, table_sem)
    to_scalars.start()
    partial[none] = jnp.zeros((tile, tile), F32)
    ask_all[me] = ask[...]
    rowsum[...] = jnp.zeros_like(rowsum)
    to_scalars.wait()

    got[me, 0] = prolong[table_s[16, me]]
    got[me, 1] = prolong[table_s[17, me]]

    @pl.when(inner)
    def _():
        send_push(0).wait_recv()
        send_push(1).wait_recv()
        face = facing(0, 0)

        def relay(to):
            low, high = bounds(to, face)
            passed[to, 0] = pushed[low]
            passed[to, 1] = pushed[high]
            send_relay(to, face).start()

        each(own, 0, 1, relay)
        each(own, 1, 0, relay)
        got[face, 0, :cut] = pushed[table_s[16, face]]
        got[face, 1, :cut] = pushed[table_s[17, face]]

    def first_product(i, _):
        load_block(i).wait()
        ph, pw = halves(prolong[i].T)
        lhs = jnp.concatenate([ph, pw, ph], axis=1)
        for k in range(0, slots, 2):
            ah, aw = halves(blocks[i, k])
            bh, bw = halves(blocks[i, k + 1])
            highs = jnp.concatenate([ah, bh], axis=1)
            rhs = jnp.concatenate([highs, highs, jnp.concatenate([aw, bw], axis=1)], axis=0)
            both = dot(lhs, rhs)
            s = i * slots + k
            partial[s] = both[:, :tile] + partial[table_s[i, k]]
            partial[s + 1] = both[:, tile:] + partial[table_s[i, k + 1]]
        return 0

    lax.fori_loop(0, rows, first_product, 0)

    spot = lax.broadcasted_iota(I32, (1, rows), 1)

    def second_product(owner):
        lhs = jnp.concatenate(
            [
                jnp.concatenate([partial[table_s[8 + c * CAP + r, owner]] for r in range(CAP)], axis=1)
                for c in range(AGD)
            ],
            axis=0,
        )
        ids = ask_all[owner][rows:]
        right = []
        for r in range(CAP):
            one = jnp.max(jnp.where(spot == table_s[16 + r, owner], ids, 0)).astype(F32)
            p = got[owner, r]
            right.append(jnp.concatenate([p * (1.0 - one), p * one], axis=1))
        rhs = jnp.concatenate(right, axis=0)
        lh, lw = halves(lhs)
        rh, rw = halves(rhs)
        prod = dot(lh, rh) + dot(lh, rw) + dot(lw, rh)
        size = jnp.abs(prod)
        rowsum[...] += size[:, :tile] + size[:, tile:]
        for c in range(AGD):
            for a in range(AGD):
                out_ref[c, owner * AGD + a] = prod[
                    c * tile : (c + 1) * tile, a * tile : (a + 1) * tile
                ]

    second_product(me)

    def collect(owner):
        send_tiles(owner, owner).wait_recv()
        second_product(owner)

    def collect_parts(owner):
        send_relay(owner, owner).wait_recv()
        send_rest(owner, owner).wait_recv()
        second_product(owner)

    @pl.when(inner)
    def _():
        each(own, 0, 1, collect)
        each(own, 1, 0, collect)

    @pl.when(outer)
    def _():
        each(own, 1, 1, collect)
        each(own, 0, 0, collect)

    each(facing, 1, 0, collect)

    @pl.when(inner)
    def _():
        send_rest(facing(0, 0), facing(0, 0)).wait_recv()

    @pl.when(outer)
    def _():
        send_relay(facing(0, 0), facing(0, 0)).wait_recv()
        send_rest(facing(0, 0), facing(0, 0)).wait_recv()

    second_product(facing(0, 0))
    each(facing, 0, 1, collect_parts)

    most = jnp.max(jnp.sum(rowsum[...], axis=1, keepdims=True), axis=0, keepdims=True)
    place_all = my_row * n + me
    peak[...] = jnp.broadcast_to(most, peak.shape)
    peaks[place_all] = jnp.broadcast_to(most, peak.shape)

    def send_peak(row, col):
        return pltpu.make_async_remote_copy(
            peak, peaks.at[place_all], peak_send, peak_recv, device_id={"row": row, "col": col}
        )

    @pl.loop(0, n)
    def _(col):
        @pl.when(col != me)
        def _():
            @pl.loop(0, m)
            def _(row):
                send_peak(row, col).start()

        @pl.when(col == me)
        def _():
            @pl.loop(1, m)
            def _(off):
                send_peak(below(off), me).start()

    others = pl.ds(0, n * m - 1)
    every = pltpu.make_async_remote_copy(
        peaks.at[others], peaks.at[others], peak_send, peak_recv, device_id={"col": across(1)}
    )

    @pl.loop(1, n)
    def _(off):
        send_ask(across(off), me).wait_send()

    def sent_whole(to):
        send_tiles(to, me).wait_send()

    def sent_rest(to):
        send_rest(to, me).wait_send()

    def sent_relay(to):
        send_relay(to, me).wait_send()

    @pl.when(inner)
    def _():
        send_push(0).wait_send()
        send_push(1).wait_send()
        each(own, 0, 1, sent_whole)
        each(own, 0, 1, sent_relay)
        each(own, 1, 0, sent_whole)
        each(own, 1, 0, sent_relay)
        each(facing, 0, 0, sent_rest)
        each(facing, 1, 0, sent_rest)

    @pl.when(outer)
    def _():
        each(own, 1, 1, sent_whole)
        each(own, 0, 0, sent_whole)
        each(facing, 0, 0, sent_whole)
        each(facing, 1, 0, sent_whole)

    every.wait_send()
    every.wait_recv()
    bound_ref[...] = jnp.broadcast_to(
        jnp.max(peaks[...], axis=0)[:1, :1] + 1e-06, bound_ref.shape
    )


def per_device(blocks, prolong, counts, columns, aggregates):
    rows, slots, tile, _ = blocks.shape
    n, m = lax.axis_size("col"), lax.axis_size("row")
    agg_row = aggregates.reshape(1, rows)
    dma = pltpu.SemaphoreType.DMA
    vmem = pl.BlockSpec(memory_space=pltpu.VMEM)
    hbm = pl.BlockSpec(memory_space=pltpu.HBM)
    galerkin, bound = pl.pallas_call(
        functools.partial(kernel, n, m),
        name="galerkin",
        out_shape=(
            jax.ShapeDtypeStruct((AGD, AGD * n, tile, tile), F32),
            jax.ShapeDtypeStruct((tile, tile), F32),
        ),
        in_specs=[hbm] * 5,
        out_specs=(vmem, vmem),
        scratch_shapes=[
            pltpu.VMEM((rows + 1, slots), I32),
            pltpu.SMEM((rows, slots), I32),
            pltpu.SMEM((1, rows), I32),
            pltpu.SMEM((1, rows), I32),
            dma((5,)),
            pltpu.VMEM((rows, slots, tile, tile), F32),
            pltpu.VMEM((rows, tile, tile), F32),
            pltpu.VMEM((rows * slots + 1, tile, tile), F32),
            pltpu.VMEM((24, 128), I32),
            pltpu.VMEM((n, CAP, tile, tile), F32),
            pltpu.VMEM((n, CAP, tile, tile), F32),
            pltpu.VMEM((rows, tile // 2, tile), F32),
            pltpu.VMEM((n, CAP, tile // 2, tile), F32),
            pltpu.VMEM((n, rows + 1, slots), I32),
            pltpu.VMEM((AGD * tile, tile), F32),
            pltpu.VMEM((1, 128), F32),
            pltpu.VMEM((n * m, 1, 128), F32),
            pltpu.SMEM((24, 128), I32),
            dma((rows,)),
            dma,
            dma,
            dma((n,)),
            dma((n,)),
            dma((n,)),
            dma((n,)),
            dma((n,)),
            dma((n,)),
            dma((2,)),
            dma((2,)),
            dma,
            dma,
            pltpu.SemaphoreType.REGULAR((2,)),
        ],
        compiler_params=pltpu.CompilerParams(
            collective_id=0, has_side_effects=True, vmem_limit_bytes=48 * 1024 * 1024
        ),
    )(*(pltpu.with_memory_space_constraint(x, pltpu.HBM) for x in (blocks, prolong, columns, agg_row, counts.reshape(1, rows))))
    return galerkin / bound


def solution(mesh):
    placed = (
        P(("row", "col"), None, None, None),
        P(("row", "col"), None, None),
        P(("row", "col")),
        P(("row", "col"), None),
        P(("row", "col")),
    )
    return jax.shard_map(
        per_device,
        mesh=mesh,
        in_specs=placed,
        out_specs=P(("row", "col"), None, None, None),
        check_vma=False,
    )
```

```python
import functools

import jax
import jax.numpy as jnp
from jax import lax
from jax.experimental import pallas as pl
from jax.experimental.pallas import tpu as pltpu
from jax.sharding import PartitionSpec as P

AGD = 2
CAP = 2
F32 = jnp.float32
BF16 = jnp.bfloat16
I32 = jnp.int32


def halves(x):
    high = x.astype(BF16)
    return high, (x - high.astype(F32)).astype(BF16)


def dot(a, b):
    return jnp.dot(a, b, preferred_element_type=F32)


def kernel(
    n, m, blocks_ref, prolong_ref, cols_ref, agg_ref, counts_ref,
    out_ref, bound_ref,
    ask, cols_s, agg_s, counts_s, small_sem,
    blocks, prolong, partial, table, sent, got, pushed, passed, ask_all, rowsum, peak, peaks, table_s,
    block_sem, prolong_sem, table_sem, ask_send, ask_recv,
    tile_send, tile_recv, relay_send, relay_recv, push_send, push_recv,
    peak_send, peak_recv, known,
):
    rows, slots = cols_s.shape
    tile = prolong.shape[-1]
    none = rows * slots
    cut = tile // 2
    lead = tile // 4
    me = lax.axis_index("col")
    my_row = lax.axis_index("row")

    width = n // 4
    line, y = me // width, lax.rem(me, width)
    side = line // 2
    outer = lax.rem(line + side, 2) == 0
    inner = lax.rem(line + side, 2) == 1

    def own(far, off):
        return jnp.where(side == 1, 2 + far, 1 - far) * width + lax.rem(y + off, width)

    def facing(far, off):
        return jnp.where(side == 1, 1 - far, 2 + far) * width + lax.rem(y + off, width)

    def across(off):
        return lax.rem(me + off, n)

    def below(off):
        return lax.rem(my_row + off, m)

    def each(where, far, first, act):
        @pl.loop(first, width)
        def _(off):
            act(where(far, off))

    barrier = pltpu.get_barrier_semaphore()

    def greet(to):
        pl.semaphore_signal(barrier, inc=1, device_id={"col": to})

    @pl.when(inner)
    def _():
        greet(facing(0, 0))
        greet(own(1, 0))

    @pl.loop(1, width)
    def _(off):
        greet(line * width + lax.rem(y + off, width))

    @pl.loop(1, m)
    def _(off):
        pl.semaphore_signal(barrier, inc=1, device_id={"row": below(off)})

    small = [
        pltpu.make_async_copy(src, dst, small_sem.at[at])
        for at, (src, dst) in enumerate(
            (
                (cols_ref, cols_s),
                (agg_ref, agg_s),
                (counts_ref, counts_s),
            )
        )
    ]
    load_prolong = pltpu.make_async_copy(prolong_ref, prolong, prolong_sem)
    load_prolong.start()
    for copy in small:
        copy.start()

    def load_block(i):
        return pltpu.make_async_copy(blocks_ref.at[i], blocks.at[i], block_sem.at[i])

    def send_ask(to, slot):
        return pltpu.make_async_remote_copy(
            ask, ask_all.at[slot], ask_send.at[to], ask_recv.at[slot], device_id={"col": to}
        )

    def send_push(part):
        some = (pl.ds(0, lead), pl.ds(lead, cut - lead))[part]
        return pltpu.make_async_remote_copy(
            prolong.at[:, some], pushed.at[:, some], push_send.at[part], push_recv.at[part],
            device_id={"col": facing(0, 0)},
        )

    def send_tiles(to, slot):
        return pltpu.make_async_remote_copy(
            sent.at[to], got.at[slot], tile_send.at[to], tile_recv.at[slot], device_id={"col": to}
        )

    def send_rest(to, slot):
        rest = pl.ds(cut, tile - cut)
        return pltpu.make_async_remote_copy(
            sent.at[to, :, rest], got.at[slot, :, rest], tile_send.at[to], tile_recv.at[slot],
            device_id={"col": to},
        )

    def send_relay(to, slot):
        return pltpu.make_async_remote_copy(
            passed.at[to], got.at[slot, :, pl.ds(0, cut)], relay_send.at[to], relay_recv.at[slot],
            device_id={"col": to},
        )

    def ask_for(to):
        send_ask(to, me).start()

    def tell(to, at):
        pl.semaphore_signal(known.at[at], inc=1, device_id={"col": to})

    pl.semaphore_wait(barrier, width + m - 1)

    @pl.when(inner)
    def _():
        tell(facing(0, 0), 1)
        load_prolong.wait()
        send_push(0).start()

    @pl.when(outer)
    def _():
        tell(own(0, 0), 0)

    for copy in small:
        copy.wait()
    at_lane = lax.broadcasted_iota(I32, ask.shape, 1)
    asking = jnp.full(ask.shape, -1, I32)
    for i in range(rows):
        for k in range(slots):
            asking = jnp.where(at_lane == i * slots + k, cols_s[i, k], asking)
        asking = jnp.where(at_lane == none + i, agg_s[0, i], asking)
    ask[...] = asking

    @pl.when(inner)
    def _():
        ask_for(facing(0, 0))
        each(own, 0, 1, ask_for)
        pl.semaphore_wait(known.at[0], 1)
        tell(facing(0, 0), 1)
        tell(own(1, 0), 0)
        each(own, 1, 0, ask_for)
        pl.semaphore_wait(known.at[1], 1)
        tell(own(1, 0), 0)
        each(facing, 0, 1, ask_for)
        pl.semaphore_wait(known.at[1], 1)
        tell(own(1, 0), 0)
        each(facing, 1, 0, ask_for)
        send_push(1).start()

    @pl.when(outer)
    def _():
        ask_for(own(0, 0))
        each(own, 1, 1, ask_for)
        pl.semaphore_wait(known.at[0], 1)
        ask_for(facing(0, 0))
        each(own, 0, 1, ask_for)
        pl.semaphore_wait(known.at[0], 1)
        each(facing, 0, 1, ask_for)
        pl.semaphore_wait(known.at[0], 1)
        each(facing, 1, 0, ask_for)

    @pl.loop(0, rows)
    def _(i):
        load_block(i).start()

    @pl.when(outer)
    def _():
        load_prolong.wait()

    def bounds(to, owner):
        asked = ask_all[to]
        mine = (asked // rows == owner) & (at_lane < none)
        within = lax.rem(asked, rows)
        return jnp.min(jnp.where(mine, within, rows - 1)), jnp.max(jnp.where(mine, within, 0))

    def reply(to):
        send_ask(to, to).wait_recv()
        low, high = bounds(to, me)
        sent[to, 0] = prolong[low]
        sent[to, 1] = prolong[high]
        send_tiles(to, me).start()

    def reply_rest(to):
        send_ask(to, to).wait_recv()
        low, high = bounds(to, me)
        sent[to, 0, cut:] = prolong[low][cut:]
        sent[to, 1, cut:] = prolong[high][cut:]
        send_rest(to, me).start()

    @pl.when(inner)
    def _():
        each(own, 0, 1, reply)
        each(own, 1, 0, reply)
        each(facing, 1, 0, reply_rest)
        each(facing, 0, 0, reply_rest)

    @pl.when(outer)
    def _():
        each(own, 1, 1, reply)
        each(own, 0, 0, reply)
        each(facing, 1, 0, reply)
        each(facing, 0, 0, reply)

    sub = lax.broadcasted_iota(I32, (8, 128), 0)
    lane = lax.broadcasted_iota(I32, (8, 128), 1)
    keys = jnp.full((8, 128), -1, I32)
    for i in range(rows):
        for k in range(slots):
            here = (sub == i) & (lane == k)
            keys = jnp.where(here, cols_s[i, k] * AGD + agg_s[0, i], keys)
    order = sub * slots + lane

    def scan_keys(i, carry):
        prev, low, high = carry
        for k in range(slots):
            col = cols_s[i, k]
            s = i * slots + k
            owner, within = col // rows, lax.rem(col, rows)
            key = jnp.where(k < counts_s[0, i], col * AGD + agg_s[0, i], -2)
            prev = jnp.where((keys == key) & (order > s), s, prev)
            low = jnp.where(lane == owner, jnp.minimum(low, within), low)
            high = jnp.where(lane == owner, jnp.maximum(high, within), high)
        return prev, low, high

    prev, low, high = lax.fori_loop(
        0, rows, scan_keys,
        (jnp.full((8, 128), none, I32), jnp.full((8, 128), rows - 1, I32), jnp.zeros((8, 128), I32)),
    )
    wanted = jnp.where(lax.rem(sub, 2) == 0, low, jnp.where(high > low, high, -1))

    def scan_last(i, last):
        for k in range(slots):
            col = cols_s[i, k]
            owner, within = col // rows, lax.rem(col, rows)
            row = jnp.where(k < counts_s[0, i], agg_s[0, i], -1)
            hit = (lane == owner) & (sub // 2 == row) & (wanted == within)
            last = jnp.where(hit, i * slots + k, last)
        return last

    last = lax.fori_loop(0, rows, scan_last, jnp.full((8, 128), none, I32))
    table[0:8, :] = prev
    table[8:16, :] = last
    table[16:24, :] = jnp.where(sub == 0, low, high)
    to_scalars = pltpu.make_async_copy(table, table_s, table_sem)
    to_scalars.start()
    partial[none] = jnp.zeros((tile, tile), F32)
    ask_all[me] = ask[...]
    rowsum[...] = jnp.zeros_like(rowsum)
    to_scalars.wait()

    got[me, 0] = prolong[table_s[16, me]]
    got[me, 1] = prolong[table_s[17, me]]

    @pl.when(inner)
    def _():
        send_push(0).wait_recv()
        send_push(1).wait_recv()
        face = facing(0, 0)

        def relay(to):
            low, high = bounds(to, face)
            passed[to, 0] = pushed[low]
            passed[to, 1] = pushed[high]
            send_relay(to, face).start()

        each(own, 0, 1, relay)
        each(own, 1, 0, relay)
        got[face, 0, :cut] = pushed[table_s[16, face]]
        got[face, 1, :cut] = pushed[table_s[17, face]]

    def first_product(i, _):
        load_block(i).wait()
        ph, pw = halves(prolong[i].T)
        lhs = jnp.concatenate([ph, pw, ph], axis=1)
        for k in range(0, slots, 2):
            ah, aw = halves(blocks[i, k])
            bh, bw = halves(blocks[i, k + 1])
            highs = jnp.concatenate([ah, bh], axis=1)
            rhs = jnp.concatenate([highs, highs, jnp.concatenate([aw, bw], axis=1)], axis=0)
            both = dot(lhs, rhs)
            s = i * slots + k
            partial[s] = both[:, :tile] + partial[table_s[i, k]]
            partial[s + 1] = both[:, tile:] + partial[table_s[i, k + 1]]
        return 0

    lax.fori_loop(0, rows, first_product, 0)

    def second_product(owner):
        lhs = jnp.concatenate(
            [
                jnp.concatenate([partial[table_s[8 + c * CAP + r, owner]] for r in range(CAP)], axis=1)
                for c in range(AGD)
            ],
            axis=0,
        )
        ids = ask_all[owner]
        right = []
        for r in range(CAP):
            one = jnp.max(jnp.where(at_lane == none + table_s[16 + r, owner], ids, 0)).astype(F32)
            p = got[owner, r]
            right.append(jnp.concatenate([p * (1.0 - one), p * one], axis=1))
        rhs = jnp.concatenate(right, axis=0)
        lh, lw = halves(lhs)
        rh, rw = halves(rhs)
        prod = dot(lh, rh) + dot(lh, rw) + dot(lw, rh)
        size = jnp.abs(prod)
        rowsum[...] += size[:, :tile] + size[:, tile:]
        for c in range(AGD):
            for a in range(AGD):
                out_ref[c, owner * AGD + a] = prod[
                    c * tile : (c + 1) * tile, a * tile : (a + 1) * tile
                ]

    second_product(me)

    def collect(owner):
        send_tiles(owner, owner).wait_recv()
        second_product(owner)

    def collect_parts(owner):
        send_relay(owner, owner).wait_recv()
        send_rest(owner, owner).wait_recv()
        second_product(owner)

    @pl.when(inner)
    def _():
        each(own, 0, 1, collect)
        each(own, 1, 0, collect)

    @pl.when(outer)
    def _():
        each(own, 1, 1, collect)
        each(own, 0, 0, collect)

    each(facing, 1, 0, collect)

    @pl.when(inner)
    def _():
        send_rest(facing(0, 0), facing(0, 0)).wait_recv()

    @pl.when(outer)
    def _():
        send_relay(facing(0, 0), facing(0, 0)).wait_recv()
        send_rest(facing(0, 0), facing(0, 0)).wait_recv()

    second_product(facing(0, 0))
    each(facing, 0, 1, collect_parts)

    most = jnp.max(jnp.sum(rowsum[...], axis=1, keepdims=True), axis=0, keepdims=True)
    place_all = my_row * n + me
    peak[...] = jnp.broadcast_to(most, peak.shape)
    peaks[place_all] = jnp.broadcast_to(most, peak.shape)

    def send_peak(row, col):
        return pltpu.make_async_remote_copy(
            peak, peaks.at[place_all], peak_send, peak_recv, device_id={"row": row, "col": col}
        )

    @pl.loop(0, n)
    def _(col):
        @pl.when(col != me)
        def _():
            @pl.loop(0, m)
            def _(row):
                send_peak(row, col).start()

        @pl.when(col == me)
        def _():
            @pl.loop(1, m)
            def _(off):
                send_peak(below(off), me).start()

    others = pl.ds(0, n * m - 1)
    every = pltpu.make_async_remote_copy(
        peaks.at[others], peaks.at[others], peak_send, peak_recv, device_id={"col": across(1)}
    )

    @pl.loop(1, n)
    def _(off):
        send_ask(across(off), me).wait_send()

    def sent_whole(to):
        send_tiles(to, me).wait_send()

    def sent_rest(to):
        send_rest(to, me).wait_send()

    def sent_relay(to):
        send_relay(to, me).wait_send()

    @pl.when(inner)
    def _():
        send_push(0).wait_send()
        send_push(1).wait_send()
        each(own, 0, 1, sent_whole)
        each(own, 0, 1, sent_relay)
        each(own, 1, 0, sent_whole)
        each(own, 1, 0, sent_relay)
        each(facing, 0, 0, sent_rest)
        each(facing, 1, 0, sent_rest)

    @pl.when(outer)
    def _():
        each(own, 1, 1, sent_whole)
        each(own, 0, 0, sent_whole)
        each(facing, 0, 0, sent_whole)
        each(facing, 1, 0, sent_whole)

    every.wait_send()
    every.wait_recv()
    bound_ref[...] = jnp.broadcast_to(
        jnp.max(peaks[...], axis=0)[:1, :1] + 1e-06, bound_ref.shape
    )


def per_device(blocks, prolong, counts, columns, aggregates):
    rows, slots, tile, _ = blocks.shape
    n, m = lax.axis_size("col"), lax.axis_size("row")
    agg_row = aggregates.reshape(1, rows)
    dma = pltpu.SemaphoreType.DMA
    vmem = pl.BlockSpec(memory_space=pltpu.VMEM)
    hbm = pl.BlockSpec(memory_space=pltpu.HBM)
    galerkin, bound = pl.pallas_call(
        functools.partial(kernel, n, m),
        name="galerkin",
        out_shape=(
            jax.ShapeDtypeStruct((AGD, AGD * n, tile, tile), F32),
            jax.ShapeDtypeStruct((tile, tile), F32),
        ),
        in_specs=[hbm] * 5,
        out_specs=(vmem, vmem),
        scratch_shapes=[
            pltpu.VMEM((1, pl.cdiv(rows * slots + rows, 128) * 128), I32),
            pltpu.SMEM((rows, slots), I32),
            pltpu.SMEM((1, rows), I32),
            pltpu.SMEM((1, rows), I32),
            dma((3,)),
            pltpu.VMEM((rows, slots, tile, tile), F32),
            pltpu.VMEM((rows, tile, tile), F32),
            pltpu.VMEM((rows * slots + 1, tile, tile), F32),
            pltpu.VMEM((24, 128), I32),
            pltpu.VMEM((n, CAP, tile, tile), F32),
            pltpu.VMEM((n, CAP, tile, tile), F32),
            pltpu.VMEM((rows, tile // 2, tile), F32),
            pltpu.VMEM((n, CAP, tile // 2, tile), F32),
            pltpu.VMEM((n, 1, pl.cdiv(rows * slots + rows, 128) * 128), I32),
            pltpu.VMEM((AGD * tile, tile), F32),
            pltpu.VMEM((1, 128), F32),
            pltpu.VMEM((n * m, 1, 128), F32),
            pltpu.SMEM((24, 128), I32),
            dma((rows,)),
            dma,
            dma,
            dma((n,)),
            dma((n,)),
            dma((n,)),
            dma((n,)),
            dma((n,)),
            dma((n,)),
            dma((2,)),
            dma((2,)),
            dma,
            dma,
            pltpu.SemaphoreType.REGULAR((2,)),
        ],
        compiler_params=pltpu.CompilerParams(
            collective_id=0, has_side_effects=True, vmem_limit_bytes=48 * 1024 * 1024
        ),
    )(*(pltpu.with_memory_space_constraint(x, pltpu.HBM) for x in (blocks, prolong, columns, agg_row, counts.reshape(1, rows))))
    return galerkin / bound


def solution(mesh):
    placed = (
        P(("row", "col"), None, None, None),
        P(("row", "col"), None, None),
        P(("row", "col")),
        P(("row", "col"), None),
        P(("row", "col")),
    )
    return jax.shard_map(
        per_device,
        mesh=mesh,
        in_specs=placed,
        out_specs=P(("row", "col"), None, None, None),
        check_vma=False,
    )
```

```python
import functools

import jax
import jax.numpy as jnp
from jax import lax
from jax.experimental import pallas as pl
from jax.experimental.pallas import tpu as pltpu
from jax.sharding import PartitionSpec as P

AGD = 2
CAP = 2
F32 = jnp.float32
BF16 = jnp.bfloat16
I32 = jnp.int32


def halves(x):
    high = x.astype(BF16)
    return high, (x - high.astype(F32)).astype(BF16)


def dot(a, b):
    return jnp.dot(a, b, preferred_element_type=F32)


def kernel(
    n, m, blocks_ref, prolong_ref, cols_ref, agg_ref, counts_ref,
    out_ref, bound_ref,
    ask, cols_s, agg_s, counts_s, small_sem,
    blocks, prolong, partial, table, sent, got, pushed, passed, ask_all, rowsum, peak, peaks, table_s,
    block_sem, prolong_sem, table_sem, ask_send, ask_recv,
    tile_send, tile_recv, relay_send, relay_recv, push_send, push_recv,
    peak_send, peak_recv, known,
):
    rows, slots = cols_s.shape
    tile = prolong.shape[-1]
    none = rows * slots
    cut = tile // 2
    lead = tile // 4
    me = lax.axis_index("col")
    my_row = lax.axis_index("row")

    width = n // 4
    line, y = me // width, lax.rem(me, width)
    side = line // 2
    outer = lax.rem(line + side, 2) == 0
    inner = lax.rem(line + side, 2) == 1

    def own(far, off):
        return jnp.where(side == 1, 2 + far, 1 - far) * width + lax.rem(y + off, width)

    def facing(far, off):
        return jnp.where(side == 1, 1 - far, 2 + far) * width + lax.rem(y + off, width)

    def across(off):
        return lax.rem(me + off, n)

    def below(off):
        return lax.rem(my_row + off, m)

    def each(where, far, first, act):
        @pl.loop(first, width)
        def _(off):
            act(where(far, off))

    barrier = pltpu.get_barrier_semaphore()

    def greet(to):
        pl.semaphore_signal(barrier, inc=1, device_id={"col": to})

    @pl.when(inner)
    def _():
        greet(facing(0, 0))
        greet(own(1, 0))

    @pl.loop(1, width)
    def _(off):
        greet(line * width + lax.rem(y + off, width))

    @pl.loop(1, m)
    def _(off):
        pl.semaphore_signal(barrier, inc=1, device_id={"row": below(off)})

    small = [
        pltpu.make_async_copy(src, dst, small_sem.at[at])
        for at, (src, dst) in enumerate(
            (
                (cols_ref, cols_s),
                (agg_ref, agg_s),
                (counts_ref, counts_s),
            )
        )
    ]
    load_prolong = pltpu.make_async_copy(prolong_ref, prolong, prolong_sem)
    load_prolong.start()
    for copy in small:
        copy.start()

    load_blocks = pltpu.make_async_copy(blocks_ref, blocks, block_sem)

    def send_ask(to, at):
        return pltpu.make_async_remote_copy(
            ask, ask_all.at[me], ask_send, ask_recv.at[at], device_id={"col": to}
        )

    def bytes_of(ref, send, recv):
        return pltpu.make_async_remote_copy(ref, ref, send, recv, device_id={"col": across(1)})

    def heard(at, count):
        bytes_of(ask_all.at[pl.ds(0, count)], ask_send, ask_recv.at[at]).wait_recv()

    def lane_of(owner):
        return lax.rem(owner, width)

    def near_at(owner):
        return 1 + lane_of(owner)

    def far_at(owner, far):
        return 1 + (1 + far) * width + lane_of(owner)

    def send_push(part):
        some = (pl.ds(0, lead), pl.ds(lead, cut - lead))[part]
        return pltpu.make_async_remote_copy(
            prolong.at[:, some], pushed.at[:, some], push_send, push_recv,
            device_id={"col": facing(0, 0)},
        )

    def send_tiles(to, slot, at):
        return pltpu.make_async_remote_copy(
            sent.at[to], got.at[slot], tile_send, tile_recv.at[at], device_id={"col": to}
        )

    def send_rest(to, slot):
        rest = pl.ds(cut, tile - cut)
        return pltpu.make_async_remote_copy(
            sent.at[to, :, rest], got.at[slot, :, rest], tile_send, tile_recv.at[far_at(slot, 0)],
            device_id={"col": to},
        )

    def send_relay(to, slot):
        return pltpu.make_async_remote_copy(
            passed.at[to], got.at[slot, :, pl.ds(0, cut)], relay_send, relay_recv, device_id={"col": to}
        )

    def ask_for(group):
        return lambda to: send_ask(to, group).start()

    def tell(to, at):
        pl.semaphore_signal(known.at[at], inc=1, device_id={"col": to})

    pl.semaphore_wait(barrier, width + m - 1)

    @pl.when(inner)
    def _():
        tell(facing(0, 0), 1)
        load_prolong.wait()
        send_push(0).start()

    @pl.when(outer)
    def _():
        tell(own(0, 0), 0)

    for copy in small:
        copy.wait()
    at_lane = lax.broadcasted_iota(I32, ask.shape, 1)
    asking = jnp.full(ask.shape, -1, I32)
    for i in range(rows):
        for k in range(slots):
            asking = jnp.where(at_lane == i * slots + k, cols_s[i, k], asking)
        asking = jnp.where(at_lane == none + i, agg_s[0, i], asking)
    ask[...] = asking

    @pl.when(inner)
    def _():
        send_ask(facing(0, 0), 1).start()
        each(own, 0, 1, ask_for(0))
        pl.semaphore_wait(known.at[0], 1)
        tell(facing(0, 0), 1)
        tell(own(1, 0), 0)
        each(own, 1, 0, ask_for(3 + y))
        pl.semaphore_wait(known.at[1], 1)
        tell(own(1, 0), 0)
        each(facing, 0, 1, ask_for(1))
        pl.semaphore_wait(known.at[1], 1)
        tell(own(1, 0), 0)
        each(facing, 1, 0, ask_for(2))
        send_push(1).start()

    @pl.when(outer)
    def _():
        send_ask(own(0, 0), 3 + y).start()
        each(own, 1, 1, ask_for(0))
        pl.semaphore_wait(known.at[0], 1)
        send_ask(facing(0, 0), 2).start()
        each(own, 0, 1, ask_for(3 + y))
        pl.semaphore_wait(known.at[0], 1)
        each(facing, 0, 1, ask_for(2))
        pl.semaphore_wait(known.at[0], 1)
        each(facing, 1, 0, ask_for(1))

    load_blocks.start()

    @pl.when(outer)
    def _():
        load_prolong.wait()

    def bounds(to, owner):
        asked = ask_all[to]
        mine = (asked // rows == owner) & (at_lane < none)
        within = lax.rem(asked, rows)
        return jnp.min(jnp.where(mine, within, rows - 1)), jnp.max(jnp.where(mine, within, 0))

    def reply(to, at):
        low, high = bounds(to, me)
        sent[to, 0] = prolong[low]
        sent[to, 1] = prolong[high]
        send_tiles(to, me, at).start()

    def reply_line(to):
        reply(to, 0)

    def reply_near(to):
        heard(3 + lane_of(to), 1)
        reply(to, near_at(me))

    def reply_far(to):
        reply(to, far_at(me, 1))

    def reply_rest(to):
        low, high = bounds(to, me)
        sent[to, 0, cut:] = prolong[low][cut:]
        sent[to, 1, cut:] = prolong[high][cut:]
        send_rest(to, me).start()

    if width > 1:
        heard(0, width - 1)

    @pl.when(inner)
    def _():
        each(own, 0, 1, reply_line)
        each(own, 1, 0, reply_near)
        heard(2, width)
        each(facing, 1, 0, reply_rest)
        heard(1, width)
        each(facing, 0, 0, reply_rest)

    @pl.when(outer)
    def _():
        each(own, 1, 1, reply_line)
        each(own, 0, 0, reply_near)
        heard(1, width)
        each(facing, 1, 0, reply_far)
        heard(2, width)
        each(facing, 0, 0, reply_far)

    sub = lax.broadcasted_iota(I32, (8, 128), 0)
    lane = lax.broadcasted_iota(I32, (8, 128), 1)
    keys = jnp.full((8, 128), -1, I32)
    for i in range(rows):
        for k in range(slots):
            here = (sub == i) & (lane == k)
            keys = jnp.where(here, cols_s[i, k] * AGD + agg_s[0, i], keys)
    order = sub * slots + lane

    def scan_keys(i, carry):
        prev, low, high = carry
        for k in range(slots):
            col = cols_s[i, k]
            s = i * slots + k
            owner, within = col // rows, lax.rem(col, rows)
            key = jnp.where(k < counts_s[0, i], col * AGD + agg_s[0, i], -2)
            prev = jnp.where((keys == key) & (order > s), s, prev)
            low = jnp.where(lane == owner, jnp.minimum(low, within), low)
            high = jnp.where(lane == owner, jnp.maximum(high, within), high)
        return prev, low, high

    prev, low, high = lax.fori_loop(
        0, rows, scan_keys,
        (jnp.full((8, 128), none, I32), jnp.full((8, 128), rows - 1, I32), jnp.zeros((8, 128), I32)),
    )
    wanted = jnp.where(lax.rem(sub, 2) == 0, low, jnp.where(high > low, high, -1))

    def scan_last(i, last):
        for k in range(slots):
            col = cols_s[i, k]
            owner, within = col // rows, lax.rem(col, rows)
            row = jnp.where(k < counts_s[0, i], agg_s[0, i], -1)
            hit = (lane == owner) & (sub // 2 == row) & (wanted == within)
            last = jnp.where(hit, i * slots + k, last)
        return last

    last = lax.fori_loop(0, rows, scan_last, jnp.full((8, 128), none, I32))
    table[0:8, :] = prev
    table[8:16, :] = last
    table[16:24, :] = jnp.where(sub == 0, low, high)
    to_scalars = pltpu.make_async_copy(table, table_s, table_sem)
    to_scalars.start()
    partial[none] = jnp.zeros((tile, tile), F32)
    ask_all[me] = ask[...]
    rowsum[...] = jnp.zeros_like(rowsum)
    to_scalars.wait()

    got[me, 0] = prolong[table_s[16, me]]
    got[me, 1] = prolong[table_s[17, me]]

    @pl.when(inner)
    def _():
        bytes_of(pushed, push_send, push_recv).wait_recv()
        face = facing(0, 0)

        def relay(to):
            low, high = bounds(to, face)
            passed[to, 0] = pushed[low]
            passed[to, 1] = pushed[high]
            send_relay(to, face).start()

        each(own, 0, 1, relay)
        each(own, 1, 0, relay)
        got[face, 0, :cut] = pushed[table_s[16, face]]
        got[face, 1, :cut] = pushed[table_s[17, face]]

    load_blocks.wait()

    def first_product(i, _):
        ph, pw = halves(prolong[i].T)
        lhs = jnp.concatenate([ph, pw, ph], axis=1)
        for k in range(0, slots, 2):
            ah, aw = halves(blocks[i, k])
            bh, bw = halves(blocks[i, k + 1])
            highs = jnp.concatenate([ah, bh], axis=1)
            rhs = jnp.concatenate([highs, highs, jnp.concatenate([aw, bw], axis=1)], axis=0)
            both = dot(lhs, rhs)
            s = i * slots + k
            partial[s] = both[:, :tile] + partial[table_s[i, k]]
            partial[s + 1] = both[:, tile:] + partial[table_s[i, k + 1]]
        return 0

    lax.fori_loop(0, rows, first_product, 0)

    def second_product(owner):
        lhs = jnp.concatenate(
            [
                jnp.concatenate([partial[table_s[8 + c * CAP + r, owner]] for r in range(CAP)], axis=1)
                for c in range(AGD)
            ],
            axis=0,
        )
        ids = ask_all[owner]
        right = []
        for r in range(CAP):
            one = jnp.max(jnp.where(at_lane == none + table_s[16 + r, owner], ids, 0)).astype(F32)
            p = got[owner, r]
            right.append(jnp.concatenate([p * (1.0 - one), p * one], axis=1))
        rhs = jnp.concatenate(right, axis=0)
        lh, lw = halves(lhs)
        rh, rw = halves(rhs)
        prod = dot(lh, rh) + dot(lh, rw) + dot(lw, rh)
        size = jnp.abs(prod)
        rowsum[...] += size[:, :tile] + size[:, tile:]
        for c in range(AGD):
            for a in range(AGD):
                out_ref[c, owner * AGD + a] = prod[
                    c * tile : (c + 1) * tile, a * tile : (a + 1) * tile
                ]

    second_product(me)

    def collect_near(owner):
        send_tiles(owner, owner, near_at(owner)).wait_recv()
        second_product(owner)

    def collect_far(owner):
        send_tiles(owner, owner, far_at(owner, 1)).wait_recv()
        second_product(owner)

    def collect_rest(owner):
        send_rest(owner, owner).wait_recv()
        second_product(owner)

    if width > 1:
        bytes_of(got.at[pl.ds(0, width - 1)], tile_send, tile_recv.at[0]).wait_recv()

    @pl.when(inner)
    def _():
        each(own, 0, 1, second_product)
        each(own, 1, 0, collect_near)
        each(facing, 1, 0, collect_far)
        if width > 1:
            bytes_of(passed.at[pl.ds(0, width - 1)], relay_send, relay_recv).wait_recv()

    @pl.when(outer)
    def _():
        each(own, 1, 1, second_product)
        collect_near(own(0, 0))
        each(facing, 1, 0, collect_far)
        each(own, 0, 1, collect_near)
        bytes_of(passed.at[pl.ds(0, width)], relay_send, relay_recv).wait_recv()

    each(facing, 0, 0, collect_rest)

    most = jnp.max(jnp.sum(rowsum[...], axis=1, keepdims=True), axis=0, keepdims=True)
    place_all = my_row * n + me
    peak[...] = jnp.broadcast_to(most, peak.shape)
    peaks[place_all] = jnp.broadcast_to(most, peak.shape)

    def send_peak(row, col):
        return pltpu.make_async_remote_copy(
            peak, peaks.at[place_all], peak_send, peak_recv, device_id={"row": row, "col": col}
        )

    @pl.loop(0, n)
    def _(col):
        @pl.when(col != me)
        def _():
            @pl.loop(0, m)
            def _(row):
                send_peak(row, col).start()

        @pl.when(col == me)
        def _():
            @pl.loop(1, m)
            def _(off):
                send_peak(below(off), me).start()

    others = pl.ds(0, n * m - 1)
    every = pltpu.make_async_remote_copy(
        peaks.at[others], peaks.at[others], peak_send, peak_recv, device_id={"col": across(1)}
    )

    bytes_of(ask_all.at[pl.ds(0, n - 1)], ask_send, ask_recv.at[0]).wait_send()

    @pl.when(inner)
    def _():
        bytes_of(pushed, push_send, push_recv).wait_send()
        bytes_of(passed.at[pl.ds(0, 2 * width - 1)], relay_send, relay_recv).wait_send()
        bytes_of(sent.at[pl.ds(0, 3 * width - 1)], tile_send, tile_recv.at[0]).wait_send()

    @pl.when(outer)
    def _():
        bytes_of(sent.at[pl.ds(0, n - 1)], tile_send, tile_recv.at[0]).wait_send()

    every.wait_send()
    every.wait_recv()
    bound_ref[...] = jnp.broadcast_to(
        jnp.max(peaks[...], axis=0)[:1, :1] + 1e-06, bound_ref.shape
    )


def per_device(blocks, prolong, counts, columns, aggregates):
    rows, slots, tile, _ = blocks.shape
    n, m = lax.axis_size("col"), lax.axis_size("row")
    agg_row = aggregates.reshape(1, rows)
    dma = pltpu.SemaphoreType.DMA
    vmem = pl.BlockSpec(memory_space=pltpu.VMEM)
    hbm = pl.BlockSpec(memory_space=pltpu.HBM)
    galerkin, bound = pl.pallas_call(
        functools.partial(kernel, n, m),
        name="galerkin",
        out_shape=(
            jax.ShapeDtypeStruct((AGD, AGD * n, tile, tile), F32),
            jax.ShapeDtypeStruct((tile, tile), F32),
        ),
        in_specs=[hbm] * 5,
        out_specs=(vmem, vmem),
        scratch_shapes=[
            pltpu.VMEM((1, pl.cdiv(rows * slots + rows, 128) * 128), I32),
            pltpu.SMEM((rows, slots), I32),
            pltpu.SMEM((1, rows), I32),
            pltpu.SMEM((1, rows), I32),
            dma((3,)),
            pltpu.VMEM((rows, slots, tile, tile), F32),
            pltpu.VMEM((rows, tile, tile), F32),
            pltpu.VMEM((rows * slots + 1, tile, tile), F32),
            pltpu.VMEM((24, 128), I32),
            pltpu.VMEM((n, CAP, tile, tile), F32),
            pltpu.VMEM((n, CAP, tile, tile), F32),
            pltpu.VMEM((rows, tile // 2, tile), F32),
            pltpu.VMEM((n, CAP, tile // 2, tile), F32),
            pltpu.VMEM((n, 1, pl.cdiv(rows * slots + rows, 128) * 128), I32),
            pltpu.VMEM((AGD * tile, tile), F32),
            pltpu.VMEM((1, 128), F32),
            pltpu.VMEM((n * m, 1, 128), F32),
            pltpu.SMEM((24, 128), I32),
            dma,
            dma,
            dma,
            dma,
            dma((3 + n // 4,)),
            dma,
            dma((1 + 3 * (n // 4),)),
            dma,
            dma,
            dma,
            dma,
            dma,
            dma,
            pltpu.SemaphoreType.REGULAR((2,)),
        ],
        compiler_params=pltpu.CompilerParams(
            collective_id=0, has_side_effects=True, vmem_limit_bytes=48 * 1024 * 1024
        ),
    )(*(pltpu.with_memory_space_constraint(x, pltpu.HBM) for x in (blocks, prolong, columns, agg_row, counts.reshape(1, rows))))
    return galerkin / bound


def solution(mesh):
    placed = (
        P(("row", "col"), None, None, None),
        P(("row", "col"), None, None),
        P(("row", "col")),
        P(("row", "col"), None),
        P(("row", "col")),
    )
    return jax.shard_map(
        per_device,
        mesh=mesh,
        in_specs=placed,
        out_specs=P(("row", "col"), None, None, None),
        check_vma=False,
    )
```

```python
import functools

import jax
import jax.numpy as jnp
from jax import lax
from jax.experimental import pallas as pl
from jax.experimental.pallas import tpu as pltpu
from jax.sharding import PartitionSpec as P

AGD = 2
CAP = 2
F32 = jnp.float32
BF16 = jnp.bfloat16
I32 = jnp.int32


def halves(x):
    high = x.astype(BF16)
    return high, (x - high.astype(F32)).astype(BF16)


def dot(a, b):
    return jnp.dot(a, b, preferred_element_type=F32)


def kernel(
    n, m, blocks_ref, prolong_ref, cols_ref, agg_ref, counts_ref,
    out_ref, bound_ref,
    ask, cols_s, agg_s, counts_s, small_sem,
    blocks, prolong, partial, table, sent, got, pushed, passed, mask, early, left, ask_all, rowsum, peak, peaks, table_s,
    block_sem, prolong_sem, table_sem, ask_send, ask_recv,
    tile_send, tile_recv, relay_send, relay_recv, push_send, push_recv,
    peak_send, peak_recv, known,
):
    rows, slots = cols_s.shape
    tile = prolong.shape[-1]
    none = rows * slots
    cut = tile // 2
    lead = tile // 4
    me = lax.axis_index("col")
    my_row = lax.axis_index("row")

    width = n // 4
    line, y = me // width, lax.rem(me, width)
    side = line // 2
    outer = lax.rem(line + side, 2) == 0
    inner = lax.rem(line + side, 2) == 1

    def own(far, off):
        return jnp.where(side == 1, 2 + far, 1 - far) * width + lax.rem(y + off, width)

    def facing(far, off):
        return jnp.where(side == 1, 1 - far, 2 + far) * width + lax.rem(y + off, width)

    def across(off):
        return lax.rem(me + off, n)

    def below(off):
        return lax.rem(my_row + off, m)

    def each(where, far, first, act):
        @pl.loop(first, width)
        def _(off):
            act(where(far, off))

    barrier = pltpu.get_barrier_semaphore()

    def greet(to):
        pl.semaphore_signal(barrier, inc=1, device_id={"col": to})

    @pl.when(inner)
    def _():
        greet(facing(0, 0))
        greet(own(1, 0))

    @pl.loop(1, width)
    def _(off):
        greet(line * width + lax.rem(y + off, width))

    @pl.loop(1, m)
    def _(off):
        pl.semaphore_signal(barrier, inc=1, device_id={"row": below(off)})

    small = [
        pltpu.make_async_copy(src, dst, small_sem.at[at])
        for at, (src, dst) in enumerate(
            (
                (cols_ref, cols_s),
                (agg_ref, agg_s),
                (counts_ref, counts_s),
            )
        )
    ]
    load_prolong = pltpu.make_async_copy(prolong_ref, prolong, prolong_sem)
    load_prolong.start()
    for copy in small:
        copy.start()

    load_blocks = pltpu.make_async_copy(blocks_ref, blocks, block_sem)

    def send_ask(to, at):
        return pltpu.make_async_remote_copy(
            ask, ask_all.at[me], ask_send, ask_recv.at[at], device_id={"col": to}
        )

    def bytes_of(ref, send, recv):
        return pltpu.make_async_remote_copy(ref, ref, send, recv, device_id={"col": across(1)})

    def heard(at, count):
        bytes_of(ask_all.at[pl.ds(0, count)], ask_send, ask_recv.at[at]).wait_recv()

    def lane_of(owner):
        return lax.rem(owner, width)

    def near_at(owner):
        return 1 + lane_of(owner)

    def far_at(owner, far):
        return 1 + (1 + far) * width + lane_of(owner)

    def send_push(part):
        some = (pl.ds(0, lead), pl.ds(lead, cut - lead))[part]
        return pltpu.make_async_remote_copy(
            prolong.at[:, some], pushed.at[:, some], push_send, push_recv,
            device_id={"col": facing(0, 0)},
        )

    def send_tiles(to, slot, at):
        return pltpu.make_async_remote_copy(
            sent.at[to], got.at[slot], tile_send, tile_recv.at[at], device_id={"col": to}
        )

    def send_rest(to, slot):
        rest = pl.ds(cut, tile - cut)
        return pltpu.make_async_remote_copy(
            sent.at[to, :, rest], got.at[slot, :, rest], tile_send, tile_recv.at[far_at(slot, 0)],
            device_id={"col": to},
        )

    def send_relay(to, slot):
        return pltpu.make_async_remote_copy(
            passed.at[to], got.at[slot, :, pl.ds(0, cut)], relay_send, relay_recv, device_id={"col": to}
        )

    def ask_for(group):
        return lambda to: send_ask(to, group).start()

    def tell(to, at):
        pl.semaphore_signal(known.at[at], inc=1, device_id={"col": to})

    pl.semaphore_wait(barrier, width + m - 1)

    @pl.when(inner)
    def _():
        tell(facing(0, 0), 1)
        load_prolong.wait()
        send_push(0).start()

    @pl.when(outer)
    def _():
        tell(own(0, 0), 0)

    for copy in small:
        copy.wait()
    at_lane = lax.broadcasted_iota(I32, ask.shape, 1)
    asking = jnp.full(ask.shape, -1, I32)
    for i in range(rows):
        for k in range(slots):
            asking = jnp.where(at_lane == i * slots + k, cols_s[i, k], asking)
        asking = jnp.where(at_lane == none + i, agg_s[0, i], asking)
    ask[...] = asking

    @pl.when(inner)
    def _():
        send_ask(facing(0, 0), 1).start()
        each(own, 0, 1, ask_for(0))
        pl.semaphore_wait(known.at[0], 1)
        tell(facing(0, 0), 1)
        tell(own(1, 0), 0)
        each(own, 1, 0, ask_for(3 + y))
        pl.semaphore_wait(known.at[1], 1)
        tell(own(1, 0), 0)
        each(facing, 0, 1, ask_for(1))
        pl.semaphore_wait(known.at[1], 1)
        tell(own(1, 0), 0)
        each(facing, 1, 0, ask_for(2))
        send_push(1).start()

    @pl.when(outer)
    def _():
        send_ask(own(0, 0), 3 + y).start()
        each(own, 1, 1, ask_for(0))
        pl.semaphore_wait(known.at[0], 1)
        send_ask(facing(0, 0), 2).start()
        each(own, 0, 1, ask_for(3 + y))
        pl.semaphore_wait(known.at[0], 1)
        each(facing, 0, 1, ask_for(2))
        pl.semaphore_wait(known.at[0], 1)
        each(facing, 1, 0, ask_for(1))

    load_blocks.start()

    @pl.when(outer)
    def _():
        load_prolong.wait()

    def bounds(to, owner):
        asked = ask_all[to]
        mine = (asked // rows == owner) & (at_lane < none)
        within = lax.rem(asked, rows)
        return jnp.min(jnp.where(mine, within, rows - 1)), jnp.max(jnp.where(mine, within, 0))

    def reply(to, at):
        low, high = bounds(to, me)
        sent[to, 0] = prolong[low]
        sent[to, 1] = prolong[high]
        send_tiles(to, me, at).start()

    def reply_line(to):
        reply(to, 0)

    def reply_near(to):
        heard(3 + lane_of(to), 1)
        reply(to, near_at(me))

    def reply_far(to):
        reply(to, far_at(me, 1))

    def reply_rest(to):
        low, high = bounds(to, me)
        sent[to, 0, cut:] = prolong[low][cut:]
        sent[to, 1, cut:] = prolong[high][cut:]
        send_rest(to, me).start()

    if width > 1:
        heard(0, width - 1)

    @pl.when(inner)
    def _():
        each(own, 0, 1, reply_line)
        each(own, 1, 0, reply_near)
        heard(2, width)
        each(facing, 1, 0, reply_rest)
        heard(1, width)
        each(facing, 0, 0, reply_rest)

    @pl.when(outer)
    def _():
        each(own, 1, 1, reply_line)
        each(own, 0, 0, reply_near)
        heard(1, width)
        each(facing, 1, 0, reply_far)
        heard(2, width)
        each(facing, 0, 0, reply_far)

    sub = lax.broadcasted_iota(I32, (8, 128), 0)
    lane = lax.broadcasted_iota(I32, (8, 128), 1)
    keys = jnp.full((8, 128), -1, I32)
    for i in range(rows):
        for k in range(slots):
            here = (sub == i) & (lane == k)
            keys = jnp.where(here, cols_s[i, k] * AGD + agg_s[0, i], keys)
    order = sub * slots + lane

    def scan_keys(i, carry):
        prev, low, high = carry
        for k in range(slots):
            col = cols_s[i, k]
            s = i * slots + k
            owner, within = col // rows, lax.rem(col, rows)
            key = jnp.where(k < counts_s[0, i], col * AGD + agg_s[0, i], -2)
            prev = jnp.where((keys == key) & (order > s), s, prev)
            low = jnp.where(lane == owner, jnp.minimum(low, within), low)
            high = jnp.where(lane == owner, jnp.maximum(high, within), high)
        return prev, low, high

    prev, low, high = lax.fori_loop(
        0, rows, scan_keys,
        (jnp.full((8, 128), none, I32), jnp.full((8, 128), rows - 1, I32), jnp.zeros((8, 128), I32)),
    )
    wanted = jnp.where(lax.rem(sub, 2) == 0, low, jnp.where(high > low, high, -1))

    def scan_last(i, last):
        for k in range(slots):
            col = cols_s[i, k]
            owner, within = col // rows, lax.rem(col, rows)
            row = jnp.where(k < counts_s[0, i], agg_s[0, i], -1)
            hit = (lane == owner) & (sub // 2 == row) & (wanted == within)
            last = jnp.where(hit, i * slots + k, last)
        return last

    last = lax.fori_loop(0, rows, scan_last, jnp.full((8, 128), none, I32))
    table[0:8, :] = prev
    table[8:16, :] = last
    table[16:24, :] = jnp.where(sub == 0, low, high)
    to_scalars = pltpu.make_async_copy(table, table_s, table_sem)
    to_scalars.start()
    partial[none] = jnp.zeros((tile, tile), F32)
    ask_all[me] = ask[...]
    rowsum[...] = jnp.zeros_like(rowsum)
    to_scalars.wait()

    got[me, 0] = prolong[table_s[16, me]]
    got[me, 1] = prolong[table_s[17, me]]

    @pl.when(inner)
    def _():
        bytes_of(pushed, push_send, push_recv).wait_recv()
        face = facing(0, 0)

        def relay(to):
            low, high = bounds(to, face)
            passed[to, 0] = pushed[low]
            passed[to, 1] = pushed[high]
            send_relay(to, face).start()

        each(own, 0, 1, relay)
        each(own, 1, 0, relay)
        got[face, 0, :cut] = pushed[table_s[16, face]]
        got[face, 1, :cut] = pushed[table_s[17, face]]

    load_blocks.wait()

    def first_product(i, _):
        ph, pw = halves(prolong[i].T)
        lhs = jnp.concatenate([ph, pw, ph], axis=1)
        for k in range(0, slots, 2):
            ah, aw = halves(blocks[i, k])
            bh, bw = halves(blocks[i, k + 1])
            highs = jnp.concatenate([ah, bh], axis=1)
            rhs = jnp.concatenate([highs, highs, jnp.concatenate([aw, bw], axis=1)], axis=0)
            both = dot(lhs, rhs)
            s = i * slots + k
            partial[s] = both[:, :tile] + partial[table_s[i, k]]
            partial[s + 1] = both[:, tile:] + partial[table_s[i, k + 1]]
        return 0

    lax.fori_loop(0, rows, first_product, 0)

    def second_product(owner):
        lhs = jnp.concatenate(
            [
                jnp.concatenate([partial[table_s[8 + c * CAP + r, owner]] for r in range(CAP)], axis=1)
                for c in range(AGD)
            ],
            axis=0,
        )
        ids = ask_all[owner]
        right = []
        for r in range(CAP):
            one = jnp.max(jnp.where(at_lane == none + table_s[16 + r, owner], ids, 0)).astype(F32)
            p = got[owner, r]
            right.append(jnp.concatenate([p * (1.0 - one), p * one], axis=1))
        rhs = jnp.concatenate(right, axis=0)
        lh, lw = halves(lhs)
        rh, rw = halves(rhs)
        prod = dot(lh, rh) + dot(lh, rw) + dot(lw, rh)
        size = jnp.abs(prod)
        rowsum[...] += size[:, :tile] + size[:, tile:]
        for c in range(AGD):
            for a in range(AGD):
                out_ref[c, owner * AGD + a] = prod[
                    c * tile : (c + 1) * tile, a * tile : (a + 1) * tile
                ]

    def three(x, y):
        return jnp.concatenate([x, y, x], axis=1)

    def deep_three(x, y):
        return jnp.concatenate([x, x, y], axis=0)

    def masked(owner, at, some):
        right = []
        for r in range(CAP):
            p = got[owner, r, some]
            right.append(jnp.concatenate([p, p], axis=1) * mask[at, r])
        return deep_three(*halves(jnp.concatenate(right, axis=0)))

    def prepare(owner):
        at = lax.rem(owner, width)
        ids = ask_all[owner]
        for r in range(CAP):
            one = jnp.max(jnp.where(at_lane == none + table_s[16 + r, owner], ids, 0)).astype(F32)
            second = (lax.broadcasted_iota(I32, (1, 2 * tile), 1) >= tile).astype(F32)
            mask[at, r] = second * one + (1.0 - second) * (1.0 - one)
        for part in range(2):
            lhs = jnp.concatenate(
                [
                    jnp.concatenate(
                        [
                            partial[table_s[8 + c * CAP + r, owner]][:, part * cut : (part + 1) * cut]
                            for r in range(CAP)
                        ],
                        axis=1,
                    )
                    for c in range(AGD)
                ],
                axis=0,
            )
            wide = three(*halves(lhs))
            if part == 0:
                early[at] = dot(wide, masked(owner, at, slice(0, cut)))
            else:
                left[at] = wide

    def finish(owner):
        at = lax.rem(owner, width)
        prod = early[at] + dot(left[at], masked(owner, at, slice(cut, tile)))
        size = jnp.abs(prod)
        rowsum[...] += size[:, :tile] + size[:, tile:]
        for c in range(AGD):
            for a in range(AGD):
                out_ref[c, owner * AGD + a] = prod[
                    c * tile : (c + 1) * tile, a * tile : (a + 1) * tile
                ]

    second_product(me)

    def collect_near(owner):
        send_tiles(owner, owner, near_at(owner)).wait_recv()
        second_product(owner)

    def collect_far(owner):
        send_tiles(owner, owner, far_at(owner, 1)).wait_recv()
        second_product(owner)

    def collect_rest(owner):
        send_rest(owner, owner).wait_recv()
        finish(owner)

    if width > 1:
        bytes_of(got.at[pl.ds(0, width - 1)], tile_send, tile_recv.at[0]).wait_recv()

    @pl.when(inner)
    def _():
        each(own, 0, 1, second_product)
        if width > 1:
            bytes_of(passed.at[pl.ds(0, width - 1)], relay_send, relay_recv).wait_recv()
        each(facing, 0, 0, prepare)
        each(own, 1, 0, collect_near)
        each(facing, 1, 0, collect_far)

    @pl.when(outer)
    def _():
        each(own, 1, 1, second_product)
        collect_near(own(0, 0))
        each(facing, 1, 0, collect_far)
        each(own, 0, 1, collect_near)
        bytes_of(passed.at[pl.ds(0, width)], relay_send, relay_recv).wait_recv()
        each(facing, 0, 0, prepare)

    each(facing, 0, 0, collect_rest)

    most = jnp.max(jnp.sum(rowsum[...], axis=1, keepdims=True), axis=0, keepdims=True)
    place_all = my_row * n + me
    peak[...] = jnp.broadcast_to(most, peak.shape)
    peaks[place_all] = jnp.broadcast_to(most, peak.shape)

    def send_peak(row, col):
        return pltpu.make_async_remote_copy(
            peak, peaks.at[place_all], peak_send, peak_recv, device_id={"row": row, "col": col}
        )

    @pl.loop(0, n)
    def _(col):
        @pl.when(col != me)
        def _():
            @pl.loop(0, m)
            def _(row):
                send_peak(row, col).start()

        @pl.when(col == me)
        def _():
            @pl.loop(1, m)
            def _(off):
                send_peak(below(off), me).start()

    others = pl.ds(0, n * m - 1)
    every = pltpu.make_async_remote_copy(
        peaks.at[others], peaks.at[others], peak_send, peak_recv, device_id={"col": across(1)}
    )

    bytes_of(ask_all.at[pl.ds(0, n - 1)], ask_send, ask_recv.at[0]).wait_send()

    @pl.when(inner)
    def _():
        bytes_of(pushed, push_send, push_recv).wait_send()
        bytes_of(passed.at[pl.ds(0, 2 * width - 1)], relay_send, relay_recv).wait_send()
        bytes_of(sent.at[pl.ds(0, 3 * width - 1)], tile_send, tile_recv.at[0]).wait_send()

    @pl.when(outer)
    def _():
        bytes_of(sent.at[pl.ds(0, n - 1)], tile_send, tile_recv.at[0]).wait_send()

    every.wait_send()
    every.wait_recv()
    bound_ref[...] = jnp.broadcast_to(
        1.0 / (jnp.max(peaks[...], axis=0)[:1, :1] + 1e-06), bound_ref.shape
    )


def per_device(blocks, prolong, counts, columns, aggregates):
    rows, slots, tile, _ = blocks.shape
    n, m = lax.axis_size("col"), lax.axis_size("row")
    agg_row = aggregates.reshape(1, rows)
    dma = pltpu.SemaphoreType.DMA
    vmem = pl.BlockSpec(memory_space=pltpu.VMEM)
    hbm = pl.BlockSpec(memory_space=pltpu.HBM)
    galerkin, bound = pl.pallas_call(
        functools.partial(kernel, n, m),
        name="galerkin",
        out_shape=(
            jax.ShapeDtypeStruct((AGD, AGD * n, tile, tile), F32),
            jax.ShapeDtypeStruct((tile, tile), F32),
        ),
        in_specs=[hbm] * 5,
        out_specs=(vmem, vmem),
        scratch_shapes=[
            pltpu.VMEM((1, pl.cdiv(rows * slots + rows, 128) * 128), I32),
            pltpu.SMEM((rows, slots), I32),
            pltpu.SMEM((1, rows), I32),
            pltpu.SMEM((1, rows), I32),
            dma((3,)),
            pltpu.VMEM((rows, slots, tile, tile), F32),
            pltpu.VMEM((rows, tile, tile), F32),
            pltpu.VMEM((rows * slots + 1, tile, tile), F32),
            pltpu.VMEM((24, 128), I32),
            pltpu.VMEM((n, CAP, tile, tile), F32),
            pltpu.VMEM((n, CAP, tile, tile), F32),
            pltpu.VMEM((rows, tile // 2, tile), F32),
            pltpu.VMEM((n, CAP, tile // 2, tile), F32),
            pltpu.VMEM((n // 4, CAP, 1, 2 * tile), F32),
            pltpu.VMEM((n // 4, AGD * tile, AGD * tile), F32),
            pltpu.VMEM((n // 4, AGD * tile, 3 * CAP * (tile // 2)), BF16),
            pltpu.VMEM((n, 1, pl.cdiv(rows * slots + rows, 128) * 128), I32),
            pltpu.VMEM((AGD * tile, tile), F32),
            pltpu.VMEM((1, 128), F32),
            pltpu.VMEM((n * m, 1, 128), F32),
            pltpu.SMEM((24, 128), I32),
            dma,
            dma,
            dma,
            dma,
            dma((3 + n // 4,)),
            dma,
            dma((1 + 3 * (n // 4),)),
            dma,
            dma,
            dma,
            dma,
            dma,
            dma,
            pltpu.SemaphoreType.REGULAR((2,)),
        ],
        compiler_params=pltpu.CompilerParams(
            collective_id=0, has_side_effects=True, vmem_limit_bytes=48 * 1024 * 1024
        ),
    )(*(pltpu.with_memory_space_constraint(x, pltpu.HBM) for x in (blocks, prolong, columns, agg_row, counts.reshape(1, rows))))
    return galerkin * bound


def solution(mesh):
    placed = (
        P(("row", "col"), None, None, None),
        P(("row", "col"), None, None),
        P(("row", "col")),
        P(("row", "col"), None),
        P(("row", "col")),
    )
    return jax.shard_map(
        per_device,
        mesh=mesh,
        in_specs=placed,
        out_specs=P(("row", "col"), None, None, None),
        check_vma=False,
    )
```

```python
import functools

import jax
import jax.numpy as jnp
from jax import lax
from jax.experimental import pallas as pl
from jax.experimental.pallas import tpu as pltpu
from jax.sharding import PartitionSpec as P

AGD = 2
CAP = 2
F32 = jnp.float32
BF16 = jnp.bfloat16
I32 = jnp.int32


def halves(x):
    high = x.astype(BF16)
    return high, (x - high.astype(F32)).astype(BF16)


def dot(a, b):
    return jnp.dot(a, b, preferred_element_type=F32)


def kernel(
    n, m, blocks_ref, prolong_ref, cols_ref, agg_ref, counts_ref,
    out_ref, bound_ref,
    ask, cols_s, agg_s, counts_s, small_sem,
    blocks, prolong, partial, table, sent, got, pushed, passed, mask, early, left, ask_all, rowsum, peak, peaks, table_s,
    block_sem, prolong_sem, table_sem, ask_send, ask_recv,
    tile_send, tile_recv, relay_send, relay_recv, push_send, push_recv,
    peak_send, peak_recv, known,
):
    rows, slots = cols_s.shape
    tile = prolong.shape[-1]
    none = rows * slots
    cut = tile // 2
    lead = tile // 4
    me = lax.axis_index("col")
    my_row = lax.axis_index("row")

    width = n // 4
    line, y = me // width, lax.rem(me, width)
    side = line // 2
    outer = lax.rem(line + side, 2) == 0
    inner = lax.rem(line + side, 2) == 1

    def own(far, off):
        return jnp.where(side == 1, 2 + far, 1 - far) * width + lax.rem(y + off, width)

    def facing(far, off):
        return jnp.where(side == 1, 1 - far, 2 + far) * width + lax.rem(y + off, width)

    def across(off):
        return lax.rem(me + off, n)

    def below(off):
        return lax.rem(my_row + off, m)

    def each(where, far, first, act):
        @pl.loop(first, width)
        def _(off):
            act(where(far, off))

    barrier = pltpu.get_barrier_semaphore()

    def greet(to):
        pl.semaphore_signal(barrier, inc=1, device_id={"col": to})

    @pl.when(inner)
    def _():
        greet(facing(0, 0))
        greet(own(1, 0))

    @pl.loop(1, width)
    def _(off):
        greet(line * width + lax.rem(y + off, width))

    @pl.loop(1, m)
    def _(off):
        pl.semaphore_signal(barrier, inc=1, device_id={"row": below(off)})

    small = [
        pltpu.make_async_copy(src, dst, small_sem.at[at])
        for at, (src, dst) in enumerate(
            (
                (cols_ref, cols_s),
                (agg_ref, agg_s),
                (counts_ref, counts_s),
            )
        )
    ]
    load_prolong = pltpu.make_async_copy(prolong_ref, prolong, prolong_sem)
    load_prolong.start()
    for copy in small:
        copy.start()

    load_blocks = pltpu.make_async_copy(blocks_ref, blocks, block_sem)

    def send_ask(to, at):
        return pltpu.make_async_remote_copy(
            ask, ask_all.at[me], ask_send, ask_recv.at[at], device_id={"col": to}
        )

    def bytes_of(ref, send, recv):
        return pltpu.make_async_remote_copy(ref, ref, send, recv, device_id={"col": across(1)})

    def heard(at, count):
        bytes_of(ask_all.at[pl.ds(0, count)], ask_send, ask_recv.at[at]).wait_recv()

    def lane_of(owner):
        return lax.rem(owner, width)

    def near_at(owner):
        return 1 + lane_of(owner)

    def far_at(owner, far):
        return 1 + (1 + far) * width + lane_of(owner)

    def send_push(part):
        some = (pl.ds(0, lead), pl.ds(lead, cut - lead))[part]
        return pltpu.make_async_remote_copy(
            prolong.at[:, some], pushed.at[:, some], push_send, push_recv,
            device_id={"col": facing(0, 0)},
        )

    def send_tiles(to, slot, at):
        return pltpu.make_async_remote_copy(
            sent.at[to], got.at[slot], tile_send, tile_recv.at[at], device_id={"col": to}
        )

    def send_rest(to, slot):
        rest = pl.ds(cut, tile - cut)
        return pltpu.make_async_remote_copy(
            sent.at[to, :, rest], got.at[slot, :, rest], tile_send, tile_recv.at[far_at(slot, 0)],
            device_id={"col": to},
        )

    def send_relay(to, slot):
        return pltpu.make_async_remote_copy(
            passed.at[to], got.at[slot, :, pl.ds(0, cut)], relay_send, relay_recv, device_id={"col": to}
        )

    def ask_for(group):
        return lambda to: send_ask(to, group).start()

    def tell(to, at):
        pl.semaphore_signal(known.at[at], inc=1, device_id={"col": to})

    pl.semaphore_wait(barrier, width + m - 1)

    @pl.when(inner)
    def _():
        load_prolong.wait()
        send_push(0).start()
        tell(facing(0, 0), 1)

    @pl.when(outer)
    def _():
        tell(own(0, 0), 0)

    for copy in small:
        copy.wait()
    at_lane = lax.broadcasted_iota(I32, ask.shape, 1)
    asking = jnp.full(ask.shape, -1, I32)
    for i in range(rows):
        for k in range(slots):
            asking = jnp.where(at_lane == i * slots + k, cols_s[i, k], asking)
        asking = jnp.where(at_lane == none + i, agg_s[0, i], asking)
    ask[...] = asking

    @pl.when(inner)
    def _():
        send_ask(facing(0, 0), 1).start()
        each(own, 0, 1, ask_for(0))
        pl.semaphore_wait(known.at[0], 1)
        tell(facing(0, 0), 1)
        tell(own(1, 0), 0)
        each(own, 1, 0, ask_for(3 + y))
        pl.semaphore_wait(known.at[1], 1)
        tell(own(1, 0), 0)
        each(facing, 0, 1, ask_for(1))
        pl.semaphore_wait(known.at[1], 1)
        tell(own(1, 0), 0)
        each(facing, 1, 0, ask_for(2))
        send_push(1).start()

    @pl.when(outer)
    def _():
        send_ask(own(0, 0), 3 + y).start()
        each(own, 1, 1, ask_for(0))
        pl.semaphore_wait(known.at[0], 1)
        send_ask(facing(0, 0), 2).start()
        each(own, 0, 1, ask_for(3 + y))
        pl.semaphore_wait(known.at[0], 1)
        each(facing, 0, 1, ask_for(2))
        pl.semaphore_wait(known.at[0], 1)
        each(facing, 1, 0, ask_for(1))

    load_blocks.start()

    @pl.when(outer)
    def _():
        load_prolong.wait()

    def bounds(to, owner):
        asked = ask_all[to]
        mine = (asked // rows == owner) & (at_lane < none)
        within = lax.rem(asked, rows)
        return jnp.min(jnp.where(mine, within, rows - 1)), jnp.max(jnp.where(mine, within, 0))

    def reply(to, at):
        low, high = bounds(to, me)
        sent[to, 0] = prolong[low]
        sent[to, 1] = prolong[high]
        send_tiles(to, me, at).start()

    def reply_line(to):
        reply(to, 0)

    def reply_near(to):
        heard(3 + lane_of(to), 1)
        reply(to, near_at(me))

    def reply_far(to):
        reply(to, far_at(me, 1))

    def reply_rest(to):
        low, high = bounds(to, me)
        sent[to, 0, cut:] = prolong[low][cut:]
        sent[to, 1, cut:] = prolong[high][cut:]
        send_rest(to, me).start()

    if width > 1:
        heard(0, width - 1)

    @pl.when(inner)
    def _():
        each(own, 0, 1, reply_line)
        each(own, 1, 0, reply_near)
        heard(2, width)
        each(facing, 1, 0, reply_rest)
        heard(1, width)
        each(facing, 0, 1, reply_rest)
        reply_rest(facing(0, 0))

    @pl.when(outer)
    def _():
        each(own, 1, 1, reply_line)
        each(own, 0, 0, reply_near)
        heard(1, width)
        each(facing, 1, 0, reply_far)
        heard(2, width)
        each(facing, 0, 0, reply_far)

    sub = lax.broadcasted_iota(I32, (8, 128), 0)
    lane = lax.broadcasted_iota(I32, (8, 128), 1)
    keys = jnp.full((8, 128), -1, I32)
    for i in range(rows):
        for k in range(slots):
            here = (sub == i) & (lane == k)
            keys = jnp.where(here, cols_s[i, k] * AGD + agg_s[0, i], keys)
    order = sub * slots + lane

    def scan_keys(i, carry):
        prev, low, high = carry
        for k in range(slots):
            col = cols_s[i, k]
            s = i * slots + k
            owner, within = col // rows, lax.rem(col, rows)
            key = jnp.where(k < counts_s[0, i], col * AGD + agg_s[0, i], -2)
            prev = jnp.where((keys == key) & (order > s), s, prev)
            low = jnp.where(lane == owner, jnp.minimum(low, within), low)
            high = jnp.where(lane == owner, jnp.maximum(high, within), high)
        return prev, low, high

    prev, low, high = lax.fori_loop(
        0, rows, scan_keys,
        (jnp.full((8, 128), none, I32), jnp.full((8, 128), rows - 1, I32), jnp.zeros((8, 128), I32)),
    )
    wanted = jnp.where(lax.rem(sub, 2) == 0, low, jnp.where(high > low, high, -1))

    def scan_last(i, last):
        for k in range(slots):
            col = cols_s[i, k]
            owner, within = col // rows, lax.rem(col, rows)
            row = jnp.where(k < counts_s[0, i], agg_s[0, i], -1)
            hit = (lane == owner) & (sub // 2 == row) & (wanted == within)
            last = jnp.where(hit, i * slots + k, last)
        return last

    last = lax.fori_loop(0, rows, scan_last, jnp.full((8, 128), none, I32))
    table[0:8, :] = prev
    table[8:16, :] = last
    table[16:24, :] = jnp.where(sub == 0, low, high)
    to_scalars = pltpu.make_async_copy(table, table_s, table_sem)
    to_scalars.start()
    partial[none] = jnp.zeros((tile, tile), F32)
    ask_all[me] = ask[...]
    rowsum[...] = jnp.zeros_like(rowsum)
    to_scalars.wait()

    got[me, 0] = prolong[table_s[16, me]]
    got[me, 1] = prolong[table_s[17, me]]

    @pl.when(inner)
    def _():
        bytes_of(pushed, push_send, push_recv).wait_recv()
        face = facing(0, 0)

        def relay(to):
            low, high = bounds(to, face)
            passed[to, 0] = pushed[low]
            passed[to, 1] = pushed[high]
            send_relay(to, face).start()

        each(own, 0, 1, relay)
        each(own, 1, 0, relay)
        got[face, 0, :cut] = pushed[table_s[16, face]]
        got[face, 1, :cut] = pushed[table_s[17, face]]

    load_blocks.wait()

    def first_product(i, _):
        ph, pw = halves(prolong[i].T)
        lhs = jnp.concatenate([ph, pw, ph], axis=1)
        for k in range(0, slots, 2):
            ah, aw = halves(blocks[i, k])
            bh, bw = halves(blocks[i, k + 1])
            highs = jnp.concatenate([ah, bh], axis=1)
            rhs = jnp.concatenate([highs, highs, jnp.concatenate([aw, bw], axis=1)], axis=0)
            both = dot(lhs, rhs)
            s = i * slots + k
            partial[s] = both[:, :tile] + partial[table_s[i, k]]
            partial[s + 1] = both[:, tile:] + partial[table_s[i, k + 1]]
        return 0

    lax.fori_loop(0, rows, first_product, 0)

    def second_product(owner):
        lhs = jnp.concatenate(
            [
                jnp.concatenate([partial[table_s[8 + c * CAP + r, owner]] for r in range(CAP)], axis=1)
                for c in range(AGD)
            ],
            axis=0,
        )
        ids = ask_all[owner]
        right = []
        for r in range(CAP):
            one = jnp.max(jnp.where(at_lane == none + table_s[16 + r, owner], ids, 0)).astype(F32)
            p = got[owner, r]
            right.append(jnp.concatenate([p * (1.0 - one), p * one], axis=1))
        rhs = jnp.concatenate(right, axis=0)
        lh, lw = halves(lhs)
        rh, rw = halves(rhs)
        prod = dot(lh, rh) + dot(lh, rw) + dot(lw, rh)
        size = jnp.abs(prod)
        rowsum[...] += size[:, :tile] + size[:, tile:]
        for c in range(AGD):
            for a in range(AGD):
                out_ref[c, owner * AGD + a] = prod[
                    c * tile : (c + 1) * tile, a * tile : (a + 1) * tile
                ]

    def three(x, y):
        return jnp.concatenate([x, y, x], axis=1)

    def deep_three(x, y):
        return jnp.concatenate([x, x, y], axis=0)

    def masked(owner, at, some):
        right = []
        for r in range(CAP):
            p = got[owner, r, some]
            right.append(jnp.concatenate([p, p], axis=1) * mask[at, r])
        return deep_three(*halves(jnp.concatenate(right, axis=0)))

    def prepare(owner):
        at = lax.rem(owner, width)
        ids = ask_all[owner]
        for r in range(CAP):
            one = jnp.max(jnp.where(at_lane == none + table_s[16 + r, owner], ids, 0)).astype(F32)
            second = (lax.broadcasted_iota(I32, (1, 2 * tile), 1) >= tile).astype(F32)
            mask[at, r] = second * one + (1.0 - second) * (1.0 - one)
        for part in range(2):
            lhs = jnp.concatenate(
                [
                    jnp.concatenate(
                        [
                            partial[table_s[8 + c * CAP + r, owner]][:, part * cut : (part + 1) * cut]
                            for r in range(CAP)
                        ],
                        axis=1,
                    )
                    for c in range(AGD)
                ],
                axis=0,
            )
            wide = three(*halves(lhs))
            if part == 0:
                early[at] = dot(wide, masked(owner, at, slice(0, cut)))
            else:
                left[at] = wide

    def finish(owner):
        at = lax.rem(owner, width)
        prod = early[at] + dot(left[at], masked(owner, at, slice(cut, tile)))
        size = jnp.abs(prod)
        rowsum[...] += size[:, :tile] + size[:, tile:]
        for c in range(AGD):
            for a in range(AGD):
                out_ref[c, owner * AGD + a] = prod[
                    c * tile : (c + 1) * tile, a * tile : (a + 1) * tile
                ]

    second_product(me)

    def collect_near(owner):
        send_tiles(owner, owner, near_at(owner)).wait_recv()
        second_product(owner)

    def collect_far(owner):
        send_tiles(owner, owner, far_at(owner, 1)).wait_recv()
        second_product(owner)

    def collect_rest(owner):
        send_rest(owner, owner).wait_recv()
        finish(owner)

    if width > 1:
        bytes_of(got.at[pl.ds(0, width - 1)], tile_send, tile_recv.at[0]).wait_recv()

    @pl.when(inner)
    def _():
        each(own, 0, 1, second_product)
        if width > 1:
            bytes_of(passed.at[pl.ds(0, width - 1)], relay_send, relay_recv).wait_recv()
        each(facing, 0, 0, prepare)
        each(own, 1, 0, collect_near)
        each(facing, 1, 0, collect_far)

    @pl.when(outer)
    def _():
        each(own, 1, 1, second_product)
        collect_near(own(0, 0))
        each(facing, 1, 0, collect_far)
        each(own, 0, 1, collect_near)
        bytes_of(passed.at[pl.ds(0, width)], relay_send, relay_recv).wait_recv()
        each(facing, 0, 0, prepare)

    each(facing, 0, 1, collect_rest)
    collect_rest(facing(0, 0))

    most = jnp.max(jnp.sum(rowsum[...], axis=1, keepdims=True), axis=0, keepdims=True)
    place_all = my_row * n + me
    peak[...] = jnp.broadcast_to(most, peak.shape)
    peaks[place_all] = jnp.broadcast_to(most, peak.shape)

    def send_peak(row, col):
        return pltpu.make_async_remote_copy(
            peak, peaks.at[place_all], peak_send, peak_recv, device_id={"row": row, "col": col}
        )

    @pl.loop(0, n)
    def _(col):
        @pl.when(col != me)
        def _():
            @pl.loop(0, m)
            def _(row):
                send_peak(row, col).start()

        @pl.when(col == me)
        def _():
            @pl.loop(1, m)
            def _(off):
                send_peak(below(off), me).start()

    others = pl.ds(0, n * m - 1)
    every = pltpu.make_async_remote_copy(
        peaks.at[others], peaks.at[others], peak_send, peak_recv, device_id={"col": across(1)}
    )

    bytes_of(ask_all.at[pl.ds(0, n - 1)], ask_send, ask_recv.at[0]).wait_send()

    @pl.when(inner)
    def _():
        bytes_of(pushed, push_send, push_recv).wait_send()
        bytes_of(passed.at[pl.ds(0, 2 * width - 1)], relay_send, relay_recv).wait_send()
        bytes_of(sent.at[pl.ds(0, 3 * width - 1)], tile_send, tile_recv.at[0]).wait_send()

    @pl.when(outer)
    def _():
        bytes_of(sent.at[pl.ds(0, n - 1)], tile_send, tile_recv.at[0]).wait_send()

    every.wait_send()
    every.wait_recv()
    bound_ref[...] = jnp.broadcast_to(
        1.0 / (jnp.max(peaks[...], axis=0)[:1, :1] + 1e-06), bound_ref.shape
    )


def per_device(blocks, prolong, counts, columns, aggregates):
    rows, slots, tile, _ = blocks.shape
    n, m = lax.axis_size("col"), lax.axis_size("row")
    agg_row = aggregates.reshape(1, rows)
    dma = pltpu.SemaphoreType.DMA
    vmem = pl.BlockSpec(memory_space=pltpu.VMEM)
    hbm = pl.BlockSpec(memory_space=pltpu.HBM)
    galerkin, bound = pl.pallas_call(
        functools.partial(kernel, n, m),
        name="galerkin",
        out_shape=(
            jax.ShapeDtypeStruct((AGD, AGD * n, tile, tile), F32),
            jax.ShapeDtypeStruct((tile, tile), F32),
        ),
        in_specs=[hbm] * 5,
        out_specs=(vmem, vmem),
        scratch_shapes=[
            pltpu.VMEM((1, pl.cdiv(rows * slots + rows, 128) * 128), I32),
            pltpu.SMEM((rows, slots), I32),
            pltpu.SMEM((1, rows), I32),
            pltpu.SMEM((1, rows), I32),
            dma((3,)),
            pltpu.VMEM((rows, slots, tile, tile), F32),
            pltpu.VMEM((rows, tile, tile), F32),
            pltpu.VMEM((rows * slots + 1, tile, tile), F32),
            pltpu.VMEM((24, 128), I32),
            pltpu.VMEM((n, CAP, tile, tile), F32),
            pltpu.VMEM((n, CAP, tile, tile), F32),
            pltpu.VMEM((rows, tile // 2, tile), F32),
            pltpu.VMEM((n, CAP, tile // 2, tile), F32),
            pltpu.VMEM((n // 4, CAP, 1, 2 * tile), F32),
            pltpu.VMEM((n // 4, AGD * tile, AGD * tile), F32),
            pltpu.VMEM((n // 4, AGD * tile, 3 * CAP * (tile // 2)), BF16),
            pltpu.VMEM((n, 1, pl.cdiv(rows * slots + rows, 128) * 128), I32),
            pltpu.VMEM((AGD * tile, tile), F32),
            pltpu.VMEM((1, 128), F32),
            pltpu.VMEM((n * m, 1, 128), F32),
            pltpu.SMEM((24, 128), I32),
            dma,
            dma,
            dma,
            dma,
            dma((3 + n // 4,)),
            dma,
            dma((1 + 3 * (n // 4),)),
            dma,
            dma,
            dma,
            dma,
            dma,
            dma,
            pltpu.SemaphoreType.REGULAR((2,)),
        ],
        compiler_params=pltpu.CompilerParams(
            collective_id=0, has_side_effects=True, vmem_limit_bytes=48 * 1024 * 1024
        ),
    )(*(pltpu.with_memory_space_constraint(x, pltpu.HBM) for x in (blocks, prolong, columns, agg_row, counts.reshape(1, rows))))
    return galerkin * bound


def solution(mesh):
    placed = (
        P(("row", "col"), None, None, None),
        P(("row", "col"), None, None),
        P(("row", "col")),
        P(("row", "col"), None),
        P(("row", "col")),
    )
    return jax.shard_map(
        per_device,
        mesh=mesh,
        in_specs=placed,
        out_specs=P(("row", "col"), None, None, None),
        check_vma=False,
    )
```

```python
import functools

import jax
import jax.numpy as jnp
from jax import lax
from jax.experimental import pallas as pl
from jax.experimental.pallas import tpu as pltpu
from jax.sharding import PartitionSpec as P

AGD = 2
CAP = 2
F32 = jnp.float32
BF16 = jnp.bfloat16
I32 = jnp.int32


def halves(x):
    high = x.astype(BF16)
    return high, (x - high.astype(F32)).astype(BF16)


def dot(a, b):
    return jnp.dot(a, b, preferred_element_type=F32)


def kernel(
    n, m, blocks_ref, prolong_ref, cols_ref, agg_ref, counts_ref,
    out_ref, bound_ref,
    ask, cols_s, agg_s, counts_s, small_sem,
    blocks, prolong, partial, table, sent, got, pushed, passed, mask, early, left, ask_all, rowsum, peak, peaks, table_s,
    block_sem, prolong_sem, table_sem, ask_send, ask_recv,
    tile_send, tile_recv, relay_send, relay_recv, push_send, push_recv,
    peak_send, peak_recv, known,
):
    rows, slots = cols_s.shape
    tile = prolong.shape[-1]
    none = rows * slots
    cut = tile // 2
    lead = tile // 4
    me = lax.axis_index("col")
    my_row = lax.axis_index("row")

    width = n // 4
    line, y = me // width, lax.rem(me, width)
    side = line // 2
    outer = lax.rem(line + side, 2) == 0
    inner = lax.rem(line + side, 2) == 1

    def own(far, off):
        return jnp.where(side == 1, 2 + far, 1 - far) * width + lax.rem(y + off, width)

    def facing(far, off):
        return jnp.where(side == 1, 1 - far, 2 + far) * width + lax.rem(y + off, width)

    def across(off):
        return lax.rem(me + off, n)

    def below(off):
        return lax.rem(my_row + off, m)

    def each(where, far, first, act):
        @pl.loop(first, width)
        def _(off):
            act(where(far, off))

    load_lead, load_tail = (
        pltpu.make_async_copy(prolong_ref.at[:, some], prolong.at[:, some], prolong_sem.at[at])
        for at, some in enumerate((pl.ds(0, lead), pl.ds(lead, tile - lead)))
    )
    load_lead.start()

    barrier = pltpu.get_barrier_semaphore()

    def greet(to):
        pl.semaphore_signal(barrier, inc=1, device_id={"col": to})

    @pl.when(inner)
    def _():
        greet(facing(0, 0))
        greet(own(1, 0))

    @pl.loop(1, width)
    def _(off):
        greet(line * width + lax.rem(y + off, width))

    @pl.loop(1, m)
    def _(off):
        pl.semaphore_signal(barrier, inc=1, device_id={"row": below(off)})

    small = [
        pltpu.make_async_copy(src, dst, small_sem.at[at])
        for at, (src, dst) in enumerate(
            (
                (cols_ref, cols_s),
                (agg_ref, agg_s),
                (counts_ref, counts_s),
            )
        )
    ]
    load_tail.start()
    for copy in small:
        copy.start()

    load_blocks = pltpu.make_async_copy(blocks_ref, blocks, block_sem)

    def send_ask(to, at):
        return pltpu.make_async_remote_copy(
            ask, ask_all.at[me], ask_send, ask_recv.at[at], device_id={"col": to}
        )

    def bytes_of(ref, send, recv):
        return pltpu.make_async_remote_copy(ref, ref, send, recv, device_id={"col": across(1)})

    def heard(at, count):
        bytes_of(ask_all.at[pl.ds(0, count)], ask_send, ask_recv.at[at]).wait_recv()

    def lane_of(owner):
        return lax.rem(owner, width)

    def near_at(owner):
        return 1 + lane_of(owner)

    def far_at(owner, far):
        return 1 + (1 + far) * width + lane_of(owner)

    def send_push(part):
        some = (pl.ds(0, lead), pl.ds(lead, cut - lead))[part]
        return pltpu.make_async_remote_copy(
            prolong.at[:, some], pushed.at[:, some], push_send, push_recv,
            device_id={"col": facing(0, 0)},
        )

    def send_tiles(to, slot, at):
        return pltpu.make_async_remote_copy(
            sent.at[to], got.at[slot], tile_send, tile_recv.at[at], device_id={"col": to}
        )

    def send_rest(to, slot):
        rest = pl.ds(cut, tile - cut)
        return pltpu.make_async_remote_copy(
            sent.at[to, :, rest], got.at[slot, :, rest], tile_send, tile_recv.at[far_at(slot, 0)],
            device_id={"col": to},
        )

    def send_relay(to, slot):
        return pltpu.make_async_remote_copy(
            passed.at[to], got.at[slot, :, pl.ds(0, cut)], relay_send, relay_recv, device_id={"col": to}
        )

    def ask_for(group):
        return lambda to: send_ask(to, group).start()

    def tell(to, at):
        pl.semaphore_signal(known.at[at], inc=1, device_id={"col": to})

    pl.semaphore_wait(barrier, width + m - 1)

    @pl.when(inner)
    def _():
        tell(facing(0, 0), 1)
        load_lead.wait()
        send_push(0).start()

    @pl.when(outer)
    def _():
        tell(own(0, 0), 0)

    for copy in small:
        copy.wait()
    at_lane = lax.broadcasted_iota(I32, ask.shape, 1)
    asking = jnp.full(ask.shape, -1, I32)
    for i in range(rows):
        for k in range(slots):
            asking = jnp.where(at_lane == i * slots + k, cols_s[i, k], asking)
        asking = jnp.where(at_lane == none + i, agg_s[0, i], asking)
    ask[...] = asking

    @pl.when(inner)
    def _():
        send_ask(facing(0, 0), 1).start()
        each(own, 0, 1, ask_for(0))
        pl.semaphore_wait(known.at[0], 1)
        tell(facing(0, 0), 1)
        tell(own(1, 0), 0)
        each(own, 1, 0, ask_for(3 + y))
        pl.semaphore_wait(known.at[1], 1)
        tell(own(1, 0), 0)
        each(facing, 0, 1, ask_for(1))
        pl.semaphore_wait(known.at[1], 1)
        tell(own(1, 0), 0)
        each(facing, 1, 0, ask_for(2))
        load_tail.wait()
        send_push(1).start()

    @pl.when(outer)
    def _():
        send_ask(own(0, 0), 3 + y).start()
        each(own, 1, 1, ask_for(0))
        pl.semaphore_wait(known.at[0], 1)
        send_ask(facing(0, 0), 2).start()
        each(own, 0, 1, ask_for(3 + y))
        pl.semaphore_wait(known.at[0], 1)
        each(facing, 0, 1, ask_for(2))
        pl.semaphore_wait(known.at[0], 1)
        each(facing, 1, 0, ask_for(1))

    load_blocks.start()

    @pl.when(outer)
    def _():
        load_lead.wait()
        load_tail.wait()

    def bounds(to, owner):
        asked = ask_all[to]
        mine = (asked // rows == owner) & (at_lane < none)
        within = lax.rem(asked, rows)
        return jnp.min(jnp.where(mine, within, rows - 1)), jnp.max(jnp.where(mine, within, 0))

    def reply(to, at):
        low, high = bounds(to, me)
        sent[to, 0] = prolong[low]
        sent[to, 1] = prolong[high]
        send_tiles(to, me, at).start()

    def reply_line(to):
        reply(to, 0)

    def reply_near(to):
        heard(3 + lane_of(to), 1)
        reply(to, near_at(me))

    def reply_far(to):
        reply(to, far_at(me, 1))

    def reply_rest(to):
        low, high = bounds(to, me)
        sent[to, 0, cut:] = prolong[low][cut:]
        sent[to, 1, cut:] = prolong[high][cut:]
        send_rest(to, me).start()

    if width > 1:
        heard(0, width - 1)

    @pl.when(inner)
    def _():
        each(own, 0, 1, reply_line)
        each(own, 1, 0, reply_near)
        heard(2, width)
        each(facing, 1, 0, reply_rest)
        heard(1, width)
        each(facing, 0, 0, reply_rest)

    @pl.when(outer)
    def _():
        each(own, 1, 1, reply_line)
        each(own, 0, 0, reply_near)
        heard(1, width)
        each(facing, 1, 0, reply_far)
        heard(2, width)
        each(facing, 0, 0, reply_far)

    sub = lax.broadcasted_iota(I32, (8, 128), 0)
    lane = lax.broadcasted_iota(I32, (8, 128), 1)
    keys = jnp.full((8, 128), -1, I32)
    for i in range(rows):
        for k in range(slots):
            here = (sub == i) & (lane == k)
            keys = jnp.where(here, cols_s[i, k] * AGD + agg_s[0, i], keys)
    order = sub * slots + lane

    def scan_keys(i, carry):
        prev, low, high = carry
        for k in range(slots):
            col = cols_s[i, k]
            s = i * slots + k
            owner, within = col // rows, lax.rem(col, rows)
            key = jnp.where(k < counts_s[0, i], col * AGD + agg_s[0, i], -2)
            prev = jnp.where((keys == key) & (order > s), s, prev)
            low = jnp.where(lane == owner, jnp.minimum(low, within), low)
            high = jnp.where(lane == owner, jnp.maximum(high, within), high)
        return prev, low, high

    prev, low, high = lax.fori_loop(
        0, rows, scan_keys,
        (jnp.full((8, 128), none, I32), jnp.full((8, 128), rows - 1, I32), jnp.zeros((8, 128), I32)),
    )
    wanted = jnp.where(lax.rem(sub, 2) == 0, low, jnp.where(high > low, high, -1))

    def scan_last(i, last):
        for k in range(slots):
            col = cols_s[i, k]
            owner, within = col // rows, lax.rem(col, rows)
            row = jnp.where(k < counts_s[0, i], agg_s[0, i], -1)
            hit = (lane == owner) & (sub // 2 == row) & (wanted == within)
            last = jnp.where(hit, i * slots + k, last)
        return last

    last = lax.fori_loop(0, rows, scan_last, jnp.full((8, 128), none, I32))
    table[0:8, :] = prev
    table[8:16, :] = last
    table[16:24, :] = jnp.where(sub == 0, low, high)
    to_scalars = pltpu.make_async_copy(table, table_s, table_sem)
    to_scalars.start()
    partial[none] = jnp.zeros((tile, tile), F32)
    ask_all[me] = ask[...]
    rowsum[...] = jnp.zeros_like(rowsum)
    to_scalars.wait()

    got[me, 0] = prolong[table_s[16, me]]
    got[me, 1] = prolong[table_s[17, me]]

    @pl.when(inner)
    def _():
        bytes_of(pushed, push_send, push_recv).wait_recv()
        face = facing(0, 0)

        def relay(to):
            low, high = bounds(to, face)
            passed[to, 0] = pushed[low]
            passed[to, 1] = pushed[high]
            send_relay(to, face).start()

        each(own, 0, 1, relay)
        each(own, 1, 0, relay)
        got[face, 0, :cut] = pushed[table_s[16, face]]
        got[face, 1, :cut] = pushed[table_s[17, face]]

    load_blocks.wait()

    def first_product(i, _):
        ph, pw = halves(prolong[i].T)
        lhs = jnp.concatenate([ph, pw, ph], axis=1)
        for k in range(0, slots, 2):
            ah, aw = halves(blocks[i, k])
            bh, bw = halves(blocks[i, k + 1])
            highs = jnp.concatenate([ah, bh], axis=1)
            rhs = jnp.concatenate([highs, highs, jnp.concatenate([aw, bw], axis=1)], axis=0)
            both = dot(lhs, rhs)
            s = i * slots + k
            partial[s] = both[:, :tile] + partial[table_s[i, k]]
            partial[s + 1] = both[:, tile:] + partial[table_s[i, k + 1]]
        return 0

    lax.fori_loop(0, rows, first_product, 0)

    def second_product(owner):
        lhs = jnp.concatenate(
            [
                jnp.concatenate([partial[table_s[8 + c * CAP + r, owner]] for r in range(CAP)], axis=1)
                for c in range(AGD)
            ],
            axis=0,
        )
        ids = ask_all[owner]
        right = []
        for r in range(CAP):
            one = jnp.max(jnp.where(at_lane == none + table_s[16 + r, owner], ids, 0)).astype(F32)
            p = got[owner, r]
            right.append(jnp.concatenate([p * (1.0 - one), p * one], axis=1))
        rhs = jnp.concatenate(right, axis=0)
        lh, lw = halves(lhs)
        rh, rw = halves(rhs)
        prod = dot(lh, rh) + dot(lh, rw) + dot(lw, rh)
        size = jnp.abs(prod)
        rowsum[...] += size[:, :tile] + size[:, tile:]
        for c in range(AGD):
            for a in range(AGD):
                out_ref[c, owner * AGD + a] = prod[
                    c * tile : (c + 1) * tile, a * tile : (a + 1) * tile
                ]

    def three(x, y):
        return jnp.concatenate([x, y, x], axis=1)

    def deep_three(x, y):
        return jnp.concatenate([x, x, y], axis=0)

    def masked(owner, at, some):
        right = []
        for r in range(CAP):
            p = got[owner, r, some]
            right.append(jnp.concatenate([p, p], axis=1) * mask[at, r])
        return deep_three(*halves(jnp.concatenate(right, axis=0)))

    def prepare(owner):
        at = lax.rem(owner, width)
        ids = ask_all[owner]
        for r in range(CAP):
            one = jnp.max(jnp.where(at_lane == none + table_s[16 + r, owner], ids, 0)).astype(F32)
            second = (lax.broadcasted_iota(I32, (1, 2 * tile), 1) >= tile).astype(F32)
            mask[at, r] = second * one + (1.0 - second) * (1.0 - one)
        for part in range(2):
            lhs = jnp.concatenate(
                [
                    jnp.concatenate(
                        [
                            partial[table_s[8 + c * CAP + r, owner]][:, part * cut : (part + 1) * cut]
                            for r in range(CAP)
                        ],
                        axis=1,
                    )
                    for c in range(AGD)
                ],
                axis=0,
            )
            wide = three(*halves(lhs))
            if part == 0:
                early[at] = dot(wide, masked(owner, at, slice(0, cut)))
            else:
                left[at] = wide

    def finish(owner):
        at = lax.rem(owner, width)
        prod = early[at] + dot(left[at], masked(owner, at, slice(cut, tile)))
        size = jnp.abs(prod)
        rowsum[...] += size[:, :tile] + size[:, tile:]
        for c in range(AGD):
            for a in range(AGD):
                out_ref[c, owner * AGD + a] = prod[
                    c * tile : (c + 1) * tile, a * tile : (a + 1) * tile
                ]

    second_product(me)

    def collect_near(owner):
        send_tiles(owner, owner, near_at(owner)).wait_recv()
        second_product(owner)

    def collect_far(owner):
        send_tiles(owner, owner, far_at(owner, 1)).wait_recv()
        second_product(owner)

    def collect_rest(owner):
        send_rest(owner, owner).wait_recv()
        finish(owner)

    if width > 1:
        bytes_of(got.at[pl.ds(0, width - 1)], tile_send, tile_recv.at[0]).wait_recv()

    @pl.when(inner)
    def _():
        each(own, 0, 1, second_product)
        if width > 1:
            bytes_of(passed.at[pl.ds(0, width - 1)], relay_send, relay_recv).wait_recv()
        each(facing, 0, 0, prepare)
        each(own, 1, 0, collect_near)
        each(facing, 1, 0, collect_far)

    @pl.when(outer)
    def _():
        each(own, 1, 1, second_product)
        collect_near(own(0, 0))
        each(facing, 1, 0, collect_far)
        each(own, 0, 1, collect_near)
        bytes_of(passed.at[pl.ds(0, width)], relay_send, relay_recv).wait_recv()
        each(facing, 0, 0, prepare)

    each(facing, 0, 0, collect_rest)

    most = jnp.max(jnp.sum(rowsum[...], axis=1, keepdims=True), axis=0, keepdims=True)
    place_all = my_row * n + me
    peak[...] = jnp.broadcast_to(most, peak.shape)
    peaks[place_all] = jnp.broadcast_to(most, peak.shape)

    def send_peak(row, col):
        return pltpu.make_async_remote_copy(
            peak, peaks.at[place_all], peak_send, peak_recv, device_id={"row": row, "col": col}
        )

    @pl.loop(0, n)
    def _(col):
        @pl.when(col != me)
        def _():
            @pl.loop(0, m)
            def _(row):
                send_peak(row, col).start()

        @pl.when(col == me)
        def _():
            @pl.loop(1, m)
            def _(off):
                send_peak(below(off), me).start()

    others = pl.ds(0, n * m - 1)
    every = pltpu.make_async_remote_copy(
        peaks.at[others], peaks.at[others], peak_send, peak_recv, device_id={"col": across(1)}
    )

    bytes_of(ask_all.at[pl.ds(0, n - 1)], ask_send, ask_recv.at[0]).wait_send()

    @pl.when(inner)
    def _():
        bytes_of(pushed, push_send, push_recv).wait_send()
        bytes_of(passed.at[pl.ds(0, 2 * width - 1)], relay_send, relay_recv).wait_send()
        bytes_of(sent.at[pl.ds(0, 3 * width - 1)], tile_send, tile_recv.at[0]).wait_send()

    @pl.when(outer)
    def _():
        bytes_of(sent.at[pl.ds(0, n - 1)], tile_send, tile_recv.at[0]).wait_send()

    every.wait_send()
    every.wait_recv()
    bound_ref[...] = jnp.broadcast_to(
        1.0 / (jnp.max(peaks[...], axis=0)[:1, :1] + 1e-06), bound_ref.shape
    )


def per_device(blocks, prolong, counts, columns, aggregates):
    rows, slots, tile, _ = blocks.shape
    n, m = lax.axis_size("col"), lax.axis_size("row")
    agg_row = aggregates.reshape(1, rows)
    dma = pltpu.SemaphoreType.DMA
    vmem = pl.BlockSpec(memory_space=pltpu.VMEM)
    hbm = pl.BlockSpec(memory_space=pltpu.HBM)
    galerkin, bound = pl.pallas_call(
        functools.partial(kernel, n, m),
        name="galerkin",
        out_shape=(
            jax.ShapeDtypeStruct((AGD, AGD * n, tile, tile), F32),
            jax.ShapeDtypeStruct((tile, tile), F32),
        ),
        in_specs=[hbm] * 5,
        out_specs=(vmem, vmem),
        scratch_shapes=[
            pltpu.VMEM((1, pl.cdiv(rows * slots + rows, 128) * 128), I32),
            pltpu.SMEM((rows, slots), I32),
            pltpu.SMEM((1, rows), I32),
            pltpu.SMEM((1, rows), I32),
            dma((3,)),
            pltpu.VMEM((rows, slots, tile, tile), F32),
            pltpu.VMEM((rows, tile, tile), F32),
            pltpu.VMEM((rows * slots + 1, tile, tile), F32),
            pltpu.VMEM((24, 128), I32),
            pltpu.VMEM((n, CAP, tile, tile), F32),
            pltpu.VMEM((n, CAP, tile, tile), F32),
            pltpu.VMEM((rows, tile // 2, tile), F32),
            pltpu.VMEM((n, CAP, tile // 2, tile), F32),
            pltpu.VMEM((n // 4, CAP, 1, 2 * tile), F32),
            pltpu.VMEM((n // 4, AGD * tile, AGD * tile), F32),
            pltpu.VMEM((n // 4, AGD * tile, 3 * CAP * (tile // 2)), BF16),
            pltpu.VMEM((n, 1, pl.cdiv(rows * slots + rows, 128) * 128), I32),
            pltpu.VMEM((AGD * tile, tile), F32),
            pltpu.VMEM((1, 128), F32),
            pltpu.VMEM((n * m, 1, 128), F32),
            pltpu.SMEM((24, 128), I32),
            dma,
            dma((2,)),
            dma,
            dma,
            dma((3 + n // 4,)),
            dma,
            dma((1 + 3 * (n // 4),)),
            dma,
            dma,
            dma,
            dma,
            dma,
            dma,
            pltpu.SemaphoreType.REGULAR((2,)),
        ],
        compiler_params=pltpu.CompilerParams(
            collective_id=0, has_side_effects=True, vmem_limit_bytes=48 * 1024 * 1024
        ),
    )(*(pltpu.with_memory_space_constraint(x, pltpu.HBM) for x in (blocks, prolong, columns, agg_row, counts.reshape(1, rows))))
    return galerkin * bound


def solution(mesh):
    placed = (
        P(("row", "col"), None, None, None),
        P(("row", "col"), None, None),
        P(("row", "col")),
        P(("row", "col"), None),
        P(("row", "col")),
    )
    return jax.shard_map(
        per_device,
        mesh=mesh,
        in_specs=placed,
        out_specs=P(("row", "col"), None, None, None),
        check_vma=False,
    )
```
